32 devices in a mesh: leaf: 8 (over z, y), rows: 4 (over x, core).
Axes of the slice: x: 2, y: 2, z: 4, core: 2. Of those that a mesh axis runs over, the one named last changes fastest.
Arguments:
- factor_zero: bfloat16 [4096, 4096], P('leaf', 'rows'), may hold values from -1 to 3, as said below
- factor_one: bfloat16 [8192, 4096], P('leaf', 'rows'), may hold values from -1 to 3, as said below
- factor_two: bfloat16 [16384, 4096], P('leaf', 'rows'), may hold values from -1 to 3, as said below
- factor_three: bfloat16 [32768, 4096], P('leaf', 'rows'), may hold values from -1 to 3, as said below
- coupling_one: bfloat16 [8192, 1, 4096], P('leaf', None, 'rows'), may hold values from -0.046875 to 0.046875
- coupling_two: bfloat16 [16384, 2, 4096], P('leaf', None, 'rows'), may hold values from -0.046875 to 0.046875
- coupling_three: bfloat16 [32768, 3, 4096], P('leaf', None, 'rows'), may hold values from -0.046875 to 0.046875
- noise_zero: bfloat16 [4096, 128], P('leaf'), may hold values from -6 to 6
- noise_one: bfloat16 [8192, 128], P('leaf'), may hold values from -6 to 6
- noise_two: bfloat16 [16384, 128], P('leaf'), may hold values from -6 to 6
- noise_three: bfloat16 [32768, 128], P('leaf'), may hold values from -6 to 6
- tail_index: int32 [16], replicated, may hold values from 0 to 127
Outputs:
- grad_zero: float32 [4096, 128], P('leaf')
- grad_one: float32 [8192, 128], P('leaf')
- grad_two: float32 [16384, 128], P('leaf')
- grad_three: float32 [32768, 128], P('leaf')
- tail_loss: float32 [], replicated
The draws below stay inside these ranges and needn't reach their ends.
Inputs may be any that keep to these rules, and one draw needn't show every extreme that they name: `factor_zero`: each 4096 x 4096 node block is lower triangular with a positive diagonal. `factor_one`: each 4096 x 4096 node block is lower triangular with a positive diagonal. `factor_two`: each 4096 x 4096 node block is lower triangular with a positive diagonal. `factor_three`: each 4096 x 4096 node block is lower triangular with a positive diagonal.
All inputs are finite; a program needn't handle non-finite values.
Results may differ from the reference program's by a relative error of at most 0.008.
Values sent between devices are 32-bit elements; how exact they have to be, the bound alone decides.
No kernel may reach another device: no remote copies, remote signals or barrier semaphores. Data moves between devices by JAX's collectives and lax.ppermute only.
A program may use at most 192 MiB of HBM per device.

```python
import jax
import jax.numpy as jnp

SEP_WIDTH = 4096
SCENARIOS = 128
LEVELS = 4
TAILS = 16


def lower_factor(key, node_count):
    first_key, second_key = jax.random.split(jax.random.fold_in(key, 17))
    total_rows = node_count * SEP_WIDTH
    row_local = (jnp.arange(total_rows, dtype=jnp.int32) % SEP_WIDTH)[:, None]
    column_ids = jnp.arange(SEP_WIDTH, dtype=jnp.int32)[None, :]
    entries = jnp.clip(jax.random.normal(first_key, (total_rows, SEP_WIDTH), jnp.float32), -4.0, 4.0) * 0.8
    diagonal = jax.random.uniform(second_key, (total_rows, 1), jnp.float32, 1.0, 2.0)
    below = (column_ids < row_local).astype(jnp.float32)
    on_diagonal = (column_ids == row_local).astype(jnp.float32)
    values = entries * below / jnp.sqrt(jnp.float32(SEP_WIDTH)) + diagonal * on_diagonal
    return values.astype(jnp.bfloat16)


def draw_factor_zero(key, part):
    return lower_factor(key, 1)


def draw_factor_one(key, part):
    return lower_factor(key, 2)


def draw_factor_two(key, part):
    return lower_factor(key, 4)


def draw_factor_three(key, part):
    return lower_factor(key, 8)


def plant(array, key, low, top_value):
    dims = array.shape
    spot = [jax.random.randint(jax.random.fold_in(key, axis), (), 0, dims[axis]) for axis in range(len(dims))]
    array = array.at[tuple(spot)].set(low)
    longest = dims.index(max(dims))
    spot[longest] = (spot[longest] + 1) % dims[longest]
    return array.at[tuple(spot)].set(top_value)


def block_scale(stream_key, dims, shards, smallest, largest):
    def one(position, blocks):
        heights = jax.random.uniform(jax.random.fold_in(jax.random.fold_in(stream_key, 6), position), (blocks,), jnp.float32, smallest / len(shards), largest / len(shards))
        return jnp.repeat(jnp.exp(heights), dims[position] // blocks).reshape((-1,) + (1,) * (len(dims) - position - 1))

    loudness = one(*shards[0])
    for cut in shards[1:]:
        loudness = loudness * one(*cut)
    return loudness


def centred(rng, extent, scale, most, shards=(), kind=jnp.bfloat16):
    drawn = jax.random.normal(rng, extent, jnp.float32) * scale
    if len(shards) > 0:
        drawn = block_scale(rng, extent, shards, -0.22, 0.18) * drawn
    return jnp.clip(drawn, min=-most, max=most).astype(kind)


def setup_inputs(seed: int = 0) -> dict:
    keys = jax.random.split(jax.random.key(seed), 13)
    return {
        "factor_zero": draw_factor_zero(jax.random.fold_in(keys[12], 71), 0),
        "factor_one": draw_factor_one(jax.random.fold_in(keys[12], 71), 0),
        "factor_two": draw_factor_two(jax.random.fold_in(keys[12], 71), 0),
        "factor_three": draw_factor_three(jax.random.fold_in(keys[12], 71), 0),
        "coupling_one": centred(keys[4], (2 * SEP_WIDTH, 1, SEP_WIDTH), (4 * SEP_WIDTH) ** -0.5, 0.046875, ((0, 8), (2, 4))),
        "coupling_two": centred(keys[5], (4 * SEP_WIDTH, 2, SEP_WIDTH), (4 * SEP_WIDTH) ** -0.5, 0.046875, ((0, 8), (2, 4))),
        "coupling_three": centred(keys[6], (8 * SEP_WIDTH, 3, SEP_WIDTH), (4 * SEP_WIDTH) ** -0.5, 0.046875, ((0, 8), (2, 4))),
        "noise_zero": centred(keys[7], (SEP_WIDTH, SCENARIOS), 1.0, 6.0, ((0, 8),)),
        "noise_one": centred(keys[8], (2 * SEP_WIDTH, SCENARIOS), 1.0, 6.0, ((0, 8),)),
        "noise_two": centred(keys[9], (4 * SEP_WIDTH, SCENARIOS), 1.0, 6.0, ((0, 8),)),
        "noise_three": centred(keys[10], (8 * SEP_WIDTH, SCENARIOS), 1.0, 6.0, ((0, 8),)),
        "tail_index": plant(jax.random.randint(keys[11], (TAILS,), 0, SCENARIOS), jax.random.fold_in(keys[11], 1), 0, SCENARIOS - 1).astype(jnp.int32),
    }


tail_level = 0.5


def reference(factor_zero, factor_one, factor_two, factor_three, coupling_one, coupling_two, coupling_three, noise_zero, noise_one, noise_two, noise_three, tail_index):
    factors = [factor_zero, factor_one, factor_two, factor_three]
    couplings = [None, coupling_one, coupling_two, coupling_three]
    noises = [noise_zero, noise_one, noise_two, noise_three]
    columns = jnp.arange(SCENARIOS, dtype=jnp.int32)
    counts = jnp.sum((tail_index[:, None] == columns[None, :]).astype(jnp.float32), axis=0)
    weights = 1.0 + counts
    rounded = {}
    cotangents = {}
    loss_sum = jnp.float32(0.0)
    for tree_level in range(LEVELS):
        for node_index in range(2 ** tree_level):
            first_row = node_index * SEP_WIDTH
            right_side = noises[tree_level][first_row:first_row + SEP_WIDTH].astype(jnp.float32)
            for ancestor in range(tree_level):
                coupling_block = couplings[tree_level][first_row:first_row + SEP_WIDTH, ancestor, :]
                parent = rounded[(ancestor, node_index >> (tree_level - ancestor))]
                right_side = right_side - jnp.dot(coupling_block, parent, preferred_element_type=jnp.float32)
            right_round = right_side.astype(jnp.bfloat16)
            factor_block = factors[tree_level][first_row:first_row + SEP_WIDTH]
            sample = jnp.dot(factor_block.T, right_round, preferred_element_type=jnp.float32)
            rounded[(tree_level, node_index)] = sample.astype(jnp.bfloat16)
            shifted = sample - tail_level
            cotangents[(tree_level, node_index)] = weights[None, :] * jax.nn.sigmoid(shifted)
            loss_sum = loss_sum + jnp.sum(weights[None, :] * jax.nn.softplus(shifted))
    solved = {}
    exact = {}
    for tree_level in reversed(range(LEVELS)):
        for node_index in range(2 ** tree_level):
            adjoint = cotangents[(tree_level, node_index)]
            for descendant in range(tree_level + 1, LEVELS):
                spread = descendant - tree_level
                for child in range(node_index << spread, (node_index + 1) << spread):
                    coupling_block = couplings[descendant][child * SEP_WIDTH:(child + 1) * SEP_WIDTH, tree_level, :]
                    adjoint = adjoint - jnp.dot(coupling_block.T, solved[(descendant, child)], preferred_element_type=jnp.float32)
            adjoint_round = adjoint.astype(jnp.bfloat16)
            first_row = node_index * SEP_WIDTH
            factor_block = factors[tree_level][first_row:first_row + SEP_WIDTH]
            result = jnp.dot(factor_block, adjoint_round, preferred_element_type=jnp.float32)
            exact[(tree_level, node_index)] = result
            solved[(tree_level, node_index)] = result.astype(jnp.bfloat16)
    gradients = [jnp.concatenate([exact[(tree_level, node_index)] for node_index in range(2 ** tree_level)], axis=0) for tree_level in range(LEVELS)]
    tail_loss = loss_sum / jnp.float32((2 ** LEVELS - 1) * SEP_WIDTH * (SCENARIOS + TAILS))
    return (gradients[0], gradients[1], gradients[2], gradients[3], tail_loss)
```

```python
import functools

import jax
import jax.numpy as jnp
from jax import lax
from jax.experimental import pallas as pl
from jax.experimental.pallas import tpu as pltpu
from jax.sharding import PartitionSpec as P

LEVELS = 4


tail_level = 0.5


def swapped(x, axis, apart):
    return lax.ppermute(x, axis, [(i, i ^ 1 << apart) for i in range(lax.axis_size(axis))])


def bits_of(axis):
    return lax.axis_size(axis).bit_length() - 1


def rows_block(count):
    return min(512, count)


def params():
    return pltpu.CompilerParams(
        dimension_semantics=("arbitrary",), vmem_limit_bytes=24 * 1024 * 1024
    )


def apply_body(has_base, half_ref, *refs):
    if has_base:
        matrix_ref, vector_ref, base_ref, out_ref = refs
    else:
        matrix_ref, vector_ref, out_ref = refs
    product = jnp.dot(matrix_ref[...], vector_ref[...], preferred_element_type=jnp.float32)
    if has_base:
        product = product + base_ref[...]
    out_ref[...] = product


def apply_rows(matrix, plane, vector, base, half, halves):
    _, rows, width = matrix.shape
    count = rows // halves
    block = rows_block(count)
    steps = count // block
    scenarios = vector.shape[1]
    in_specs = [
        pl.BlockSpec((pl.Squeezed(), block, width), lambda i, h: (plane, h[0] * steps + i, 0)),
        pl.BlockSpec((width, scenarios), lambda i, h: (0, 0)),
    ]
    operands = [matrix, vector]
    if base is not None:
        in_specs.append(pl.BlockSpec((block, scenarios), lambda i, h: (h[0] * steps + i, 0)))
        operands.append(base)
    return pl.pallas_call(
        functools.partial(apply_body, base is not None),
        out_shape=jax.ShapeDtypeStruct((count, scenarios), jnp.float32),
        grid_spec=pltpu.PrefetchScalarGridSpec(
            num_scalar_prefetch=1,
            grid=(steps,),
            in_specs=in_specs,
            out_specs=pl.BlockSpec((block, scenarios), lambda i, h: (i, 0)),
        ),
        compiler_params=params(),
    )(half, *operands)


def first_body(half_ref, matrix_ref, noise_ref, out_ref, total_ref):
    step = pl.program_id(0)

    @pl.when(step == 0)
    def _():
        total_ref[...] = jnp.zeros_like(total_ref)

    total_ref[...] += lax.dot_general(
        noise_ref[...], matrix_ref[...], (((0,), (0,)), ((), ())), preferred_element_type=jnp.float32
    )

    @pl.when(step == pl.num_programs(0) - 1)
    def _():
        out_ref[...] = total_ref[...].T


def sample_body(half_steps, half_ref, matrix_ref, noise_ref, own_ref, other_ref, out_ref, total_ref):
    step = pl.program_id(0)

    @pl.when(step == 0)
    def _():
        total_ref[...] = jnp.zeros_like(total_ref)

    def add(terms_ref):
        right = (noise_ref[...].astype(jnp.float32) - terms_ref[...]).astype(jnp.bfloat16)
        total_ref[...] += lax.dot_general(
            right, matrix_ref[...], (((0,), (0,)), ((), ())), preferred_element_type=jnp.float32
        )

    @pl.when(step < half_steps)
    def _():
        add(own_ref)

    @pl.when(step >= half_steps)
    def _():
        add(other_ref)

    @pl.when(step == pl.num_programs(0) - 1)
    def _():
        out_ref[...] = total_ref[...].T


def sample_rows(matrix, noise, own, other, half):
    rows, width = matrix.shape
    scenarios = noise.shape[1]
    if own is None:
        block = rows_block(rows)
        steps = rows // block
        place = lambda i, h: (i, 0)
        body = first_body
        in_specs = [pl.BlockSpec((block, width), place), pl.BlockSpec((block, scenarios), place)]
        operands = [matrix, noise]
    else:
        block = rows_block(rows // 2)
        half_steps = rows // 2 // block
        steps = 2 * half_steps
        place = lambda i, h: ((h[0] * half_steps + i) % steps, 0)
        body = functools.partial(sample_body, half_steps)
        in_specs = [
            pl.BlockSpec((block, width), place),
            pl.BlockSpec((block, scenarios), place),
            pl.BlockSpec((block, scenarios), lambda i, h: (jnp.minimum(i, half_steps - 1), 0)),
            pl.BlockSpec((block, scenarios), lambda i, h: (jnp.maximum(i - half_steps, 0), 0)),
        ]
        operands = [matrix, noise, own, other]
    return pl.pallas_call(
        body,
        out_shape=jax.ShapeDtypeStruct((width, scenarios), jnp.float32),
        grid_spec=pltpu.PrefetchScalarGridSpec(
            num_scalar_prefetch=1,
            grid=(steps,),
            in_specs=in_specs,
            out_specs=pl.BlockSpec((width, scenarios), lambda i, h: (0, 0)),
            scratch_shapes=[pltpu.VMEM((scenarios, width), jnp.float32)],
        ),
        compiler_params=params(),
    )(half, *operands)


def gather_body(half_steps, half_ref, matrix_ref, own_ref, other_ref, out_ref, exact_ref, round_ref, total_ref):
    step = pl.program_id(0)

    @pl.when(step == 0)
    def _():
        total_ref[...] = jnp.zeros_like(total_ref)

    def add(terms_ref):
        exact = terms_ref[...]
        exact_ref[...] = exact
        short = exact.astype(jnp.bfloat16)
        round_ref[...] = short
        total_ref[...] += lax.dot_general(
            short, matrix_ref[...], (((0,), (0,)), ((), ())), preferred_element_type=jnp.float32
        )

    @pl.when(step < half_steps)
    def _():
        add(own_ref)

    @pl.when(step >= half_steps)
    def _():
        add(other_ref)

    @pl.when(step == pl.num_programs(0) - 1)
    def _():
        out_ref[...] = total_ref[...].T


def gather_rows(matrix, plane, own, other, half):
    _, rows, width = matrix.shape
    scenarios = own.shape[1]
    block = rows_block(rows // 2)
    half_steps = rows // 2 // block
    steps = 2 * half_steps
    place = lambda i, h: ((h[0] * half_steps + i) % steps, 0)
    return pl.pallas_call(
        functools.partial(gather_body, half_steps),
        out_shape=(
            jax.ShapeDtypeStruct((width, scenarios), jnp.float32),
            jax.ShapeDtypeStruct((rows, scenarios), jnp.float32),
            jax.ShapeDtypeStruct((rows, scenarios), jnp.bfloat16),
        ),
        grid_spec=pltpu.PrefetchScalarGridSpec(
            num_scalar_prefetch=1,
            grid=(steps,),
            in_specs=[
                pl.BlockSpec(
                    (pl.Squeezed(), block, width), lambda i, h: (plane, (h[0] * half_steps + i) % steps, 0)
                ),
                pl.BlockSpec((block, scenarios), lambda i, h: (jnp.minimum(i, half_steps - 1), 0)),
                pl.BlockSpec((block, scenarios), lambda i, h: (jnp.maximum(i - half_steps, 0), 0)),
            ],
            out_specs=(
                pl.BlockSpec((width, scenarios), lambda i, h: (0, 0)),
                pl.BlockSpec((block, scenarios), place),
                pl.BlockSpec((block, scenarios), place),
            ),
            scratch_shapes=[pltpu.VMEM((scenarios, width), jnp.float32)],
        ),
        compiler_params=params(),
    )(half, matrix, own, other)


def later_body(has_base, matrix_ref, vector_ref, *refs):
    if has_base:
        base_ref, out_ref, total_ref = refs
    else:
        out_ref, total_ref = refs
    step = pl.program_id(0)

    @pl.when(step == 0)
    def _():
        total_ref[...] = jnp.zeros_like(total_ref)

    total_ref[...] += lax.dot_general(
        vector_ref[...], matrix_ref[...], (((0,), (0,)), ((), ())), preferred_element_type=jnp.float32
    )

    @pl.when(step == pl.num_programs(0) - 1)
    def _():
        total = total_ref[...].T
        if has_base:
            total = total + base_ref[...]
        out_ref[...] = total


def later_rows(matrix, plane, vector, base):
    _, rows, width = matrix.shape
    scenarios = vector.shape[1]
    block = rows_block(rows)
    in_specs = [
        pl.BlockSpec((pl.Squeezed(), block, width), lambda i: (plane, i, 0)),
        pl.BlockSpec((block, scenarios), lambda i: (i, 0)),
    ]
    operands = [matrix, vector]
    if base is not None:
        in_specs.append(pl.BlockSpec((width, scenarios), lambda i: (0, 0)))
        operands.append(base)
    return pl.pallas_call(
        functools.partial(later_body, base is not None),
        out_shape=jax.ShapeDtypeStruct((width, scenarios), jnp.float32),
        grid_spec=pltpu.PrefetchScalarGridSpec(
            num_scalar_prefetch=0,
            grid=(rows // block,),
            in_specs=in_specs,
            out_specs=pl.BlockSpec((width, scenarios), lambda i: (0, 0)),
            scratch_shapes=[pltpu.VMEM((scenarios, width), jnp.float32)],
        ),
        compiler_params=params(),
    )(*operands)


def rows_sum(sent, kept):
    own = kept + swapped(sent, "rows", 0)
    for position in range(1, bits_of("rows")):
        own = own + swapped(own, "rows", position)
    return own, swapped(own, "rows", 0)


def halve(value, position, leaf_index):
    half_rows = value.shape[0] // 2
    upper = leaf_index >> position & 1
    kept = lax.dynamic_slice_in_dim(value, upper * half_rows, half_rows, 0)
    sent = lax.dynamic_slice_in_dim(value, (1 - upper) * half_rows, half_rows, 0)
    return kept + swapped(sent, "leaf", position)


def double(value, position, leaf_index):
    partner = swapped(value, "leaf", position)
    upper = leaf_index >> position & 1
    return jnp.where(
        upper == 1,
        jnp.concatenate([partner, value], axis=0),
        jnp.concatenate([value, partner], axis=0),
    )


def group_sum(value, group_bits, leaf_index):
    if group_bits == 0:
        return value
    if group_bits == 1:
        return value + swapped(value, "leaf", 0)
    if group_bits == 2:
        middle = value.shape[0] // 2
        first, second = value[:middle], value[middle:]
        first_got = swapped(first, "leaf", 0)
        second_got = swapped(second, "leaf", 1)
        first, second = first + first_got, second + second_got
        first_got = swapped(first, "leaf", 1)
        second_got = swapped(second, "leaf", 0)
        return jnp.concatenate([first + first_got, second + second_got], axis=0)
    for position in range(2):
        value = halve(value, position, leaf_index)
    for position in range(2, group_bits):
        value = value + swapped(value, "leaf", position)
    for position in reversed(range(2)):
        value = double(value, position, leaf_index)
    return value


def total_sum(value):
    for axis in ("leaf", "rows"):
        for position in range(bits_of(axis)):
            value = value + swapped(value, axis, position)
    return value


def on_device(
    factor_zero,
    factor_one,
    factor_two,
    factor_three,
    coupling_one,
    coupling_two,
    coupling_three,
    noise_zero,
    noise_one,
    noise_two,
    noise_three,
    tail_index,
):
    factors = [factor_zero, factor_one, factor_two, factor_three]
    couplings = [None] + [
        jnp.transpose(coupling, (1, 0, 2)) for coupling in (coupling_one, coupling_two, coupling_three)
    ]
    noises = [noise_zero, noise_one, noise_two, noise_three]
    leaf_bits = bits_of("leaf")
    leaf_index = lax.axis_index("leaf")
    core = (lax.axis_index("rows") & 1).astype(jnp.int32)
    keep_half = core.reshape(1)
    send_half = (1 - core).reshape(1)
    whole = jnp.zeros((1,), jnp.int32)
    full_width = factor_zero.shape[1] * lax.axis_size("rows")
    scenario_count = noise_zero.shape[1]
    columns = jnp.arange(scenario_count, dtype=jnp.int32)
    counts = jnp.sum((tail_index[:, None] == columns[None, :]).astype(jnp.float32), axis=0)
    weights = 1.0 + counts
    samples = []
    early = [None] * LEVELS
    loss_rows = jnp.zeros((8, scenario_count), jnp.float32)
    for tree_level in range(LEVELS):
        group_bits = leaf_bits - tree_level
        own = other = None
        if tree_level > 0:
            coupling = couplings[tree_level]
            last = samples[-1].astype(jnp.bfloat16)
            sent = apply_rows(coupling, tree_level - 1, last, early[tree_level], send_half, 2)
            kept = apply_rows(coupling, tree_level - 1, last, early[tree_level], keep_half, 2)
            own, other = rows_sum(sent, kept)
            for deeper in range(tree_level + 1, LEVELS):
                early[deeper] = apply_rows(
                    couplings[deeper], tree_level - 1, last, early[deeper], whole, 1
                )
        partial_sample = sample_rows(factors[tree_level], noises[tree_level], own, other, keep_half)
        sample = group_sum(partial_sample, group_bits, leaf_index)
        samples.append(sample)
        piece_rows = sample.shape[0] >> group_bits
        member = leaf_index & (1 << group_bits) - 1
        own_rows = lax.dynamic_slice_in_dim(sample, member * piece_rows, piece_rows, 0)
        losses = weights[None, :] * jax.nn.softplus(own_rows - tail_level)
        loss_rows = loss_rows + jnp.sum(losses.reshape(-1, 8, scenario_count), axis=0)
    loss_total = jnp.sum(total_sum(loss_rows))
    tail_loss = loss_total / jnp.float32(
        (2**LEVELS - 1) * full_width * (scenario_count + tail_index.shape[0])
    )
    pending = [None] * LEVELS
    gradients = [None] * LEVELS
    for tree_level in reversed(range(LEVELS)):
        group_bits = leaf_bits - tree_level
        adjoint = weights[None, :] * jax.nn.sigmoid(samples[tree_level] - tail_level)
        if tree_level < LEVELS - 1:
            adjoint = adjoint - group_sum(pending[tree_level], group_bits, leaf_index)
        adjoint_round = adjoint.astype(jnp.bfloat16)
        factor = factors[tree_level][None]
        sent = apply_rows(factor, 0, adjoint_round, None, send_half, 2)
        kept = apply_rows(factor, 0, adjoint_round, None, keep_half, 2)
        own, other = rows_sum(sent, kept)
        if tree_level > 0:
            upward, gradients[tree_level], solved = gather_rows(
                couplings[tree_level], tree_level - 1, own, other, keep_half
            )
            before = pending[tree_level - 1]
            pending[tree_level - 1] = upward if before is None else before + upward
            for ancestor in range(tree_level - 1):
                pending[ancestor] = later_rows(
                    couplings[tree_level], ancestor, solved, pending[ancestor]
                )
        else:
            gradients[0] = jnp.where(
                core == 1,
                jnp.concatenate([other, own], axis=0),
                jnp.concatenate([own, other], axis=0),
            )
    return (gradients[0], gradients[1], gradients[2], gradients[3], tail_loss)


def solution(mesh):
    in_specs = (
        P("leaf", "rows"),
        P("leaf", "rows"),
        P("leaf", "rows"),
        P("leaf", "rows"),
        P("leaf", None, "rows"),
        P("leaf", None, "rows"),
        P("leaf", None, "rows"),
        P("leaf", None),
        P("leaf", None),
        P("leaf", None),
        P("leaf", None),
        P(),
    )
    out_specs = (P("leaf", None), P("leaf", None), P("leaf", None), P("leaf", None), P())
    return jax.shard_map(
        on_device, mesh=mesh, in_specs=in_specs, out_specs=out_specs, check_vma=False
    )
```

```python
import functools

import jax
import jax.numpy as jnp
from jax import lax
from jax.experimental import pallas as pl
from jax.experimental.pallas import tpu as pltpu
from jax.sharding import PartitionSpec as P

LEVELS = 4


tail_level = 0.5


def swapped(x, axis, apart):
    return lax.ppermute(x, axis, [(i, i ^ 1 << apart) for i in range(lax.axis_size(axis))])


def bits_of(axis):
    return lax.axis_size(axis).bit_length() - 1


VMEM = pl.BlockSpec(memory_space=pltpu.VMEM)
HBM = pl.BlockSpec(memory_space=pltpu.HBM)
SMEM = pl.BlockSpec(memory_space=pltpu.SMEM)


def in_hbm(array):
    return pltpu.with_memory_space_constraint(array, pltpu.HBM)


def in_vmem(array):
    return pltpu.with_memory_space_constraint(array, pltpu.VMEM)


def kernel_params():
    return pltpu.CompilerParams(vmem_limit_bytes=14 * 1024 * 1024)


def cost(rows, width, scenarios):
    return pl.CostEstimate(flops=scenarios, transcendentals=0, bytes_accessed=scenarios)


def block_rows(rows):
    return min(rows, max(128, rows // 4))


def block_count(rows):
    return rows // block_rows(rows)


def stream(matrix_ref, plane, first, rows, buffer_ref, base, sems, sem_base):
    block = block_rows(rows)
    copies = []
    for number in range(rows // block):
        start = first + number * block
        if not isinstance(start, int):
            start = pl.multiple_of(start, block)
        copy = pltpu.make_async_copy(
            matrix_ref.at[plane, pl.ds(start, block), :],
            buffer_ref.at[pl.ds(base + number * block, block), :],
            sems.at[sem_base + number],
        )
        copy.start()
        copies.append((copy, number * block, block))
    return copies


def across(left, right):
    return lax.dot_general(left, right, (((0,), (0,)), ((), ())), preferred_element_type=jnp.float32)


def added(total, part):
    return part if total is None else total + part


def apply_body(plane, count, has_base, unit_ref, matrix_ref, vector_ref, *refs):
    out_ref, buffer_ref, sems = refs[-3:]
    start = pl.multiple_of(unit_ref[0] * count, count)
    for copy, offset, block in stream(matrix_ref, plane, start, count, buffer_ref, 0, sems, 0):
        copy.wait()
        rows = slice(offset, offset + block)
        product = jnp.dot(buffer_ref[rows, :], vector_ref[...], preferred_element_type=jnp.float32)
        if has_base:
            product = product + refs[0][pl.ds(pl.multiple_of(start + offset, block), block), :]
        out_ref[rows, :] = product


def apply_rows(matrix, plane, vector, base, unit, units):
    _, rows, width = matrix.shape
    count = rows // units
    scenarios = vector.shape[1]
    operands = [in_hbm(matrix), in_vmem(vector)] + ([] if base is None else [in_vmem(base)])
    return pl.pallas_call(
        functools.partial(apply_body, plane, count, base is not None),
        out_shape=pltpu.VMEM((count, scenarios), jnp.float32),
        in_specs=[SMEM, HBM] + [VMEM] * (len(operands) - 1),
        out_specs=VMEM,
        scratch_shapes=[
            pltpu.VMEM((count, width), jnp.bfloat16),
            pltpu.SemaphoreType.DMA((block_count(count),)),
        ],
        compiler_params=kernel_params(),
        cost_estimate=cost(count, width, scenarios),
    )(unit.reshape(1), *operands)


def start_body(matrix_ref, noise_ref, out_ref, buffer_ref, right_ref, sems, right_sem):
    rows = buffer_ref.shape[0]
    noise_copy = pltpu.make_async_copy(noise_ref, right_ref, right_sem.at[0])
    noise_copy.start()
    copies = stream(matrix_ref, 0, 0, rows, buffer_ref, 0, sems, 0)
    noise_copy.wait()
    total = None
    for copy, offset, block in copies:
        copy.wait()
        part = slice(offset, offset + block)
        total = added(total, across(right_ref[part, :], buffer_ref[part, :]))
    out_ref[...] = total.T


def start_rows(matrix, noise):
    rows, width = matrix.shape[1:]
    scenarios = noise.shape[1]
    return pl.pallas_call(
        start_body,
        out_shape=pltpu.VMEM((width, scenarios), jnp.float32),
        in_specs=[HBM, HBM],
        out_specs=VMEM,
        scratch_shapes=[
            pltpu.VMEM((rows, width), jnp.bfloat16),
            pltpu.VMEM((rows, scenarios), jnp.bfloat16),
            pltpu.SemaphoreType.DMA((block_count(rows),)),
            pltpu.SemaphoreType.DMA((1,)),
        ],
        compiler_params=kernel_params(),
        cost_estimate=cost(rows, width, scenarios),
    )(in_hbm(matrix), in_hbm(noise))


def sample_body(count, first, has_base, last, half_ref, matrix_ref, noise_ref, own_ref, other_ref, *refs):
    out_ref, buffer_ref, right_ref, sems, right_sems = refs[-5:]
    blocks = block_count(count)
    parts = ((own_ref, half_ref[0]), (other_ref, 1 - half_ref[0]))
    started = []
    for number, (_, half) in enumerate(parts):
        start = pl.multiple_of((first + half) * count, count)
        noise_copy = pltpu.make_async_copy(
            noise_ref.at[pl.ds(start, count), :],
            right_ref.at[pl.ds(number * count, count), :],
            right_sems.at[number],
        )
        noise_copy.start()
        copies = stream(
            matrix_ref, 0, start, count, buffer_ref, number * count, sems, number * blocks
        )
        started.append((noise_copy, copies))
    total = refs[0][...] if has_base else None
    for number, (terms_ref, _) in enumerate(parts):
        noise_copy, copies = started[number]
        noise_copy.wait()
        for copy, offset, block in copies:
            copy.wait()
            held = slice(number * count + offset, number * count + offset + block)
            noise = right_ref[held, :].astype(jnp.float32)
            right = (noise - terms_ref[offset:offset + block, :]).astype(jnp.bfloat16)
            total = added(total, across(right, buffer_ref[held, :]))
    out_ref[...] = total.T if last else total


def sample_rows(matrix, noise, own, other, half, chunk, chunks, base):
    _, rows, width = matrix.shape
    scenarios = noise.shape[1]
    count = rows // chunks // 2
    operands = [in_hbm(matrix), in_hbm(noise), in_vmem(own), in_vmem(other)]
    if base is not None:
        operands.append(in_vmem(base))
    last = chunk == chunks - 1
    shape = (width, scenarios) if last else (scenarios, width)
    return pl.pallas_call(
        functools.partial(sample_body, count, 2 * chunk, base is not None, last),
        out_shape=pltpu.VMEM(shape, jnp.float32),
        in_specs=[SMEM, HBM, HBM] + [VMEM] * (len(operands) - 2),
        out_specs=VMEM,
        scratch_shapes=[
            pltpu.VMEM((2 * count, width), jnp.bfloat16),
            pltpu.VMEM((2 * count, scenarios), jnp.bfloat16),
            pltpu.SemaphoreType.DMA((2 * block_count(count),)),
            pltpu.SemaphoreType.DMA((2,)),
        ],
        compiler_params=kernel_params(),
        cost_estimate=cost(2 * count, width, scenarios),
    )(half.reshape(1), *operands)


def gather_body(plane, count, first, has_base, last, half_ref, matrix_ref, own_ref, other_ref, *refs):
    out_ref, short_ref, exact_ref, buffer_ref, sems, exact_sems = refs[-6:]
    blocks = block_count(count)
    parts = ((own_ref, half_ref[0]), (other_ref, 1 - half_ref[0]))
    started = []
    for number, (_, half) in enumerate(parts):
        start = pl.multiple_of((first + half) * count, count)
        started.append(
            stream(matrix_ref, plane, start, count, buffer_ref, number * count, sems, number * blocks)
        )
    exact_copies = []
    for number, (terms_ref, half) in enumerate(parts):
        start = pl.multiple_of((first + half) * count, count)
        copy = pltpu.make_async_copy(terms_ref, exact_ref.at[pl.ds(start, count), :], exact_sems.at[number])
        copy.start()
        exact_copies.append(copy)
    total = refs[0][...] if has_base else None
    for number, (terms_ref, half) in enumerate(parts):
        for copy, offset, block in started[number]:
            copy.wait()
            short = terms_ref[offset:offset + block, :].astype(jnp.bfloat16)
            place = pl.multiple_of(half * count + offset, block)
            short_ref[pl.ds(place, block), :] = short
            held = slice(number * count + offset, number * count + offset + block)
            total = added(total, across(short, buffer_ref[held, :]))
    out_ref[...] = total.T if last else total
    for copy in exact_copies:
        copy.wait()


def gather_rows(matrix, plane, own, other, half, chunk, chunks, base, exact):
    _, rows, width = matrix.shape
    scenarios = own.shape[1]
    count = rows // chunks // 2
    operands = [in_hbm(matrix), in_vmem(own), in_vmem(other)]
    in_specs = [SMEM, HBM, VMEM, VMEM]
    aliases = {}
    if base is not None:
        operands += [in_vmem(base), in_hbm(exact)]
        in_specs += [VMEM, HBM]
        aliases = {5: 2}
    last = chunk == chunks - 1
    shape = (width, scenarios) if last else (scenarios, width)
    return pl.pallas_call(
        functools.partial(gather_body, plane, count, 2 * chunk, base is not None, last),
        out_shape=(
            pltpu.VMEM(shape, jnp.float32),
            pltpu.VMEM((2 * count, scenarios), jnp.bfloat16),
            pltpu.HBM((rows, scenarios), jnp.float32),
        ),
        in_specs=in_specs,
        out_specs=(VMEM, VMEM, HBM),
        scratch_shapes=[
            pltpu.VMEM((2 * count, width), jnp.bfloat16),
            pltpu.SemaphoreType.DMA((2 * block_count(count),)),
            pltpu.SemaphoreType.DMA((2,)),
        ],
        input_output_aliases=aliases,
        compiler_params=kernel_params(),
        cost_estimate=cost(2 * count, width, scenarios),
    )(half.reshape(1), *operands)


def place_body(count, half_ref, own_ref, other_ref, exact_ref, sems):
    copies = []
    for number, (terms_ref, half) in enumerate(((own_ref, half_ref[0]), (other_ref, 1 - half_ref[0]))):
        start = pl.multiple_of(half * count, count)
        copies.append(
            pltpu.make_async_copy(terms_ref, exact_ref.at[pl.ds(start, count), :], sems.at[number])
        )
    for copy in copies:
        copy.start()
    for copy in copies:
        copy.wait()


def place_rows(own, other, half):
    count, scenarios = own.shape
    return pl.pallas_call(
        functools.partial(place_body, count),
        out_shape=pltpu.HBM((2 * count, scenarios), jnp.float32),
        in_specs=[SMEM, VMEM, VMEM],
        out_specs=HBM,
        scratch_shapes=[pltpu.SemaphoreType.DMA((2,))],
        compiler_params=kernel_params(),
    )(half.reshape(1), in_vmem(own), in_vmem(other))


def later_body(plane, count, has_base, matrix_ref, *refs):
    out_ref, buffer_ref, sems = refs[-3:]
    each = refs[0].shape[0]
    total = None
    for copy, offset, block in stream(matrix_ref, plane, 0, buffer_ref.shape[0], buffer_ref, 0, sems, 0):
        copy.wait()
        inner = offset % each
        short = refs[offset // each][inner:inner + block, :]
        total = added(total, across(short, buffer_ref[offset:offset + block, :]))
    total = total.T
    if has_base:
        total = total + refs[count][...]
    out_ref[...] = total


def later_rows(matrix, plane, shorts, base):
    _, rows, width = matrix.shape
    scenarios = shorts[0].shape[1]
    operands = [in_vmem(operand) for operand in list(shorts) + ([] if base is None else [base])]
    return pl.pallas_call(
        functools.partial(later_body, plane, len(shorts), base is not None),
        out_shape=pltpu.VMEM((width, scenarios), jnp.float32),
        in_specs=[HBM] + [VMEM] * len(operands),
        out_specs=VMEM,
        scratch_shapes=[
            pltpu.VMEM((rows, width), jnp.bfloat16),
            pltpu.SemaphoreType.DMA((block_count(rows),)),
        ],
        compiler_params=kernel_params(),
        cost_estimate=cost(rows, width, scenarios),
    )(in_hbm(matrix), *operands)


def tied(first, second):
    return lax.optimization_barrier((first, second))


def run_jobs(jobs, inputs):
    return [job[1](given) for job, given in zip(jobs, inputs)]


def keep_results(jobs, results):
    for job, result in zip(jobs, results):
        job[2](result)


class Waits:
    def __init__(self):
        self.queue = []

    def put(self, *jobs):
        self.queue.append(list(jobs))

    def take(self):
        return self.queue.pop(0) if self.queue else []

    def drain(self):
        for jobs in self.queue:
            for job in jobs:
                job[2](job[1](job[0]()))
        self.queue = []


def exchanges(values, axis_positions, jobs=()):
    inputs = [job[0]() for job in jobs]
    values, inputs = tied(list(values), inputs)
    got = [swapped(value, axis, position) for value, (axis, position) in zip(values, axis_positions)]
    got, results = tied(got, run_jobs(jobs, inputs))
    keep_results(jobs, results)
    return values, got


def exchange(value, axis, position, jobs=()):
    values, got = exchanges([value], [(axis, position)], jobs)
    return values[0], got[0]


def halve(value, position, leaf_index, jobs):
    half_rows = value.shape[0] // 2
    upper = leaf_index >> position & 1
    kept = lax.dynamic_slice_in_dim(value, upper * half_rows, half_rows, 0)
    sent = lax.dynamic_slice_in_dim(value, (1 - upper) * half_rows, half_rows, 0)
    _, got = exchange(sent, "leaf", position, jobs)
    return kept + got


def double(value, position, leaf_index, jobs):
    value, partner = exchange(value, "leaf", position, jobs)
    upper = leaf_index >> position & 1
    return jnp.where(
        upper == 1,
        jnp.concatenate([partner, value], axis=0),
        jnp.concatenate([value, partner], axis=0),
    )


def group_sum(value, group_bits, leaf_index, waits):
    if group_bits == 0:
        return value
    if group_bits == 1:
        value, got = exchange(value, "leaf", 0, waits.take())
        return value + got
    if group_bits == 2:
        middle = value.shape[0] // 2
        parts = [value[:middle], value[middle:]]
        for positions in ((0, 1), (1, 0)):
            parts, got = exchanges(parts, [("leaf", position) for position in positions], waits.take())
            parts = [part + more for part, more in zip(parts, got)]
        return jnp.concatenate(parts, axis=0)
    for position in range(2):
        value = halve(value, position, leaf_index, waits.take())
    for position in range(2, group_bits):
        value, got = exchange(value, "leaf", position, waits.take())
        value = value + got
    for position in reversed(range(2)):
        value = double(value, position, leaf_index, waits.take())
    return value


def chunks_of(rows):
    return 2 if rows >= 4096 else 1


def rows_stage(produce, consume, chunks, core, waits):
    bits = bits_of("rows")
    owns = []
    for chunk in range(chunks):
        sent = produce(2 * chunk + 1 - core, owns[-1] if owns else None)
        kept = []
        job = (lambda: (), lambda _: produce(2 * chunk + core, sent), kept.append)
        _, got = exchange(sent, "rows", 0, [job])
        owns.append(kept[0] + got)
    state = None
    if chunks == 1:
        own = owns[0]
        for position in range(1, bits):
            own, got = exchange(own, "rows", position, waits.take())
            own = own + got
        return consume(0, own, swapped(own, "rows", 0), None)
    gots = [swapped(own, "rows", 1) for own in owns]
    jobs = waits.take()
    owns[-1], inputs = tied(owns[-1], [job[0]() for job in jobs])
    gots[0], results = tied(gots[0], run_jobs(jobs, inputs))
    keep_results(jobs, results)
    for chunk in range(chunks):
        own = owns[chunk]
        got = gots[chunk]
        if chunk + 1 < chunks:
            got, owns[chunk + 1] = tied(got, owns[chunk + 1])
        elif state is not None:
            got, state = tied(got, state)
        own = own + got
        for position in range(2, bits):
            own = own + swapped(own, "rows", position)
        state = consume(chunk, own, swapped(own, "rows", 0), state)
    return state


def on_device(
    factor_zero,
    factor_one,
    factor_two,
    factor_three,
    coupling_one,
    coupling_two,
    coupling_three,
    noise_zero,
    noise_one,
    noise_two,
    noise_three,
    tail_index,
):
    factors = [factor[None] for factor in (factor_zero, factor_one, factor_two, factor_three)]
    noises = [noise_zero, noise_one, noise_two, noise_three]
    couplings = {
        1: [jnp.transpose(coupling_one, (1, 0, 2))],
        2: [],
        3: [jnp.transpose(coupling_three, (1, 0, 2))],
    }
    leaf_bits = bits_of("leaf")
    leaf_index = lax.axis_index("leaf")
    core = (lax.axis_index("rows") & 1).astype(jnp.int32)
    width = factor_zero.shape[1]
    full_width = width * lax.axis_size("rows")
    scenario_count = noise_zero.shape[1]
    columns = jnp.arange(scenario_count, dtype=jnp.int32)
    counts = jnp.sum((tail_index[:, None] == columns[None, :]).astype(jnp.float32), axis=0)
    weights = 1.0 + counts

    early = {}

    def turn_job():
        return (lambda: coupling_two, lambda given: jnp.transpose(given, (1, 0, 2)), couplings[2].append)

    def early_job(level, plane, vector):
        def run(given):
            return apply_rows(couplings[level][0], plane, given, early.get(level), jnp.int32(0), 1)

        return (lambda: vector, run, lambda result: early.__setitem__(level, result))

    def work(*steps):
        waits = Waits()
        for jobs in steps:
            waits.put(*jobs)
        return waits

    samples = []
    for tree_level in range(LEVELS):
        group_bits = leaf_bits - tree_level
        if tree_level == 0:
            part = start_rows(factors[0], noises[0])
        else:
            plane = tree_level - 1
            last = samples[-1].astype(jnp.bfloat16)
            if tree_level == 1:
                waits = work([turn_job()])
            elif tree_level == 2:
                waits = work([early_job(3, 1, last)])
            else:
                waits = work()
            chunks = chunks_of(factors[tree_level].shape[1])

            def produce(unit, after):
                vector = last
                if after is not None:
                    vector, _ = tied(vector, after)
                return apply_rows(
                    couplings[tree_level][0], plane, vector, early.get(tree_level), unit, 2 * chunks
                )

            def consume(chunk, own, other, state):
                return sample_rows(factors[tree_level], noises[tree_level], own, other, core, chunk, chunks, state)

            part = rows_stage(produce, consume, chunks, core, waits)
        if tree_level == 0:
            waits = work()
        elif tree_level == 1:
            waits = work(
                [early_job(3, 0, last)],
                [early_job(2, 0, last)],
            )
        else:
            waits = work()
        samples.append(group_sum(part, group_bits, leaf_index, waits))
        waits.drain()

    losses = []

    def loss_job(given):
        total = jnp.zeros((8, scenario_count), jnp.float32)
        for tree_level in range(LEVELS):
            group_bits = leaf_bits - tree_level
            piece_rows = given[tree_level].shape[0] >> group_bits
            member = leaf_index & (1 << group_bits) - 1
            own_rows = lax.dynamic_slice_in_dim(given[tree_level], member * piece_rows, piece_rows, 0)
            terms = weights[None, :] * jax.nn.softplus(own_rows - tail_level)
            total = total + jnp.sum(terms.reshape(-1, 8, scenario_count), axis=0)
        return total

    steps = [("leaf", position) for position in range(leaf_bits)]
    steps += [("rows", position) for position in range(bits_of("rows"))]

    def sum_job(count):
        def run(given):
            for _ in range(count):
                if steps:
                    axis, position = steps.pop(0)
                    given = given + swapped(given, axis, position)
            return given

        return (lambda: losses[-1], run, losses.append)

    pending = [None] * LEVELS
    gradients = [None] * LEVELS

    def later_job(level, plane):
        def run(given):
            return later_rows(couplings[level][0], plane, given, pending[plane])

        return (lambda: shorts[level], run, lambda result: pending.__setitem__(plane, result))

    shorts = {}
    loss_start = (lambda: samples, loss_job, losses.append)
    for tree_level in reversed(range(LEVELS)):
        group_bits = leaf_bits - tree_level
        adjoint = weights[None, :] * jax.nn.sigmoid(samples[tree_level] - tail_level)
        if tree_level < LEVELS - 1:
            if tree_level == 2:
                waits = work(
                    [
                        later_job(3, 1), later_job(3, 0),
                    ]
                )
            elif tree_level == 1:
                waits = work(
                    [later_job(2, 0)], [sum_job(1)]
                )
            else:
                waits = work([sum_job(1)])
            adjoint = adjoint - group_sum(pending[tree_level], group_bits, leaf_index, waits)
            waits.drain()
        adjoint_round = adjoint.astype(jnp.bfloat16)
        chunks = chunks_of(factors[tree_level].shape[1])
        if tree_level == 3:
            waits = work([loss_start])
        elif tree_level == 2:
            waits = work([sum_job(2)])
        elif tree_level == 1:
            waits = work([sum_job(1)])
        else:
            waits = work()

        def produce(unit, after):
            vector = adjoint_round
            if after is not None:
                vector, _ = tied(vector, after)
            return apply_rows(factors[tree_level], 0, vector, None, unit, 2 * chunks)

        shorts[tree_level] = []

        def consume(chunk, own, other, state):
            if tree_level == 0:
                return place_rows(own, other, core)
            base, exact = (None, None) if state is None else state
            out, short, exact = gather_rows(
                couplings[tree_level][0], tree_level - 1, own, other, core, chunk, chunks, base, exact
            )
            shorts[tree_level].append(short)
            return out, exact

        result = rows_stage(produce, consume, chunks, core, waits)
        if tree_level == 0:
            gradients[0] = result
            continue
        upward, gradients[tree_level] = result
        before = pending[tree_level - 1]
        pending[tree_level - 1] = upward if before is None else before + upward
    while steps:
        last_sum = sum_job(1)
        last_sum[2](last_sum[1](last_sum[0]()))
    tail_loss = jnp.sum(losses[-1]) / jnp.float32(
        (2**LEVELS - 1) * full_width * (scenario_count + tail_index.shape[0])
    )
    return (gradients[0], gradients[1], gradients[2], gradients[3], tail_loss)


def solution(mesh):
    in_specs = (
        P("leaf", "rows"),
        P("leaf", "rows"),
        P("leaf", "rows"),
        P("leaf", "rows"),
        P("leaf", None, "rows"),
        P("leaf", None, "rows"),
        P("leaf", None, "rows"),
        P("leaf", None),
        P("leaf", None),
        P("leaf", None),
        P("leaf", None),
        P(),
    )
    out_specs = (P("leaf", None), P("leaf", None), P("leaf", None), P("leaf", None), P())
    return jax.shard_map(
        on_device, mesh=mesh, in_specs=in_specs, out_specs=out_specs, check_vma=False
    )
```

```python
import functools

import jax
import jax.numpy as jnp
from jax import lax
from jax.experimental import pallas as pl
from jax.experimental.pallas import tpu as pltpu
from jax.sharding import PartitionSpec as P

LEVELS = 4


tail_level = 0.5


def swapped(x, axis, apart):
    return lax.ppermute(x, axis, [(i, i ^ 1 << apart) for i in range(lax.axis_size(axis))])


def bits_of(axis):
    return lax.axis_size(axis).bit_length() - 1


VMEM = pl.BlockSpec(memory_space=pltpu.VMEM)
HBM = pl.BlockSpec(memory_space=pltpu.HBM)


def in_hbm(array):
    return pltpu.with_memory_space_constraint(array, pltpu.HBM)


def in_vmem(array):
    return pltpu.with_memory_space_constraint(array, pltpu.VMEM)


def kernel_params():
    return pltpu.CompilerParams(vmem_limit_bytes=14 * 1024 * 1024)


def cost(rows, width, scenarios):
    return pl.CostEstimate(flops=scenarios, transcendentals=0, bytes_accessed=scenarios)


def block_rows(rows):
    return min(rows, max(128, rows // 4))


def first_row(chunk, side, count):
    if side is None:
        return chunk * count
    low = lax.axis_index("rows") & 1
    return (2 * chunk + (low if side == 0 else 1 - low)) * count


def block_copy(matrix_ref, plane, first, block, number, buffer_ref, base, sems, sem_base):
    start = pl.multiple_of(first + number * block, block)
    place = pl.multiple_of(base + number * block, block)
    return pltpu.make_async_copy(
        matrix_ref.at[plane, pl.ds(start, block), :],
        buffer_ref.at[pl.ds(place, block), :],
        sems.at[sem_base + number],
    )


def apply_body(plane, chunk, side, count, has_base, matrix_ref, vector_ref, *refs):
    start = first_row(chunk, side, count)
    if plane is None:
        rows = pl.ds(pl.multiple_of(start, count), count)
        product = jnp.dot(matrix_ref[rows, :], vector_ref[...], preferred_element_type=jnp.float32)
        if has_base:
            product = product + refs[0][rows, :]
        refs[-1][...] = product
        return
    out_ref, buffer_ref, sems = refs[-3:]
    block = block_rows(count)
    blocks = count // block
    for number in range(blocks):
        block_copy(matrix_ref, plane, start, block, number, buffer_ref, 0, sems, 0).start()

    def step(number, carry):
        block_copy(matrix_ref, plane, start, block, number, buffer_ref, 0, sems, 0).wait()
        rows = pl.ds(pl.multiple_of(number * block, block), block)
        product = jnp.dot(buffer_ref[rows, :], vector_ref[...], preferred_element_type=jnp.float32)
        if has_base:
            product = product + refs[0][pl.ds(pl.multiple_of(start + number * block, block), block), :]
        out_ref[rows, :] = product
        return carry

    lax.fori_loop(0, blocks, step, 0)


def apply_rows(matrix, plane, vector, base, chunk, side, chunks):
    rows, width = matrix.shape[-2:]
    count = rows // chunks if side is None else rows // chunks // 2
    scenarios = vector.shape[1]
    held = plane is None
    operands = [in_vmem(matrix) if held else in_hbm(matrix), in_vmem(vector)]
    operands += [] if base is None else [in_vmem(base)]
    return pl.pallas_call(
        functools.partial(apply_body, plane, chunk, side, count, base is not None),
        out_shape=pltpu.VMEM((count, scenarios), jnp.float32),
        in_specs=[VMEM if held else HBM] + [VMEM] * (len(operands) - 1),
        out_specs=VMEM,
        scratch_shapes=[]
        if held
        else [
            pltpu.VMEM((count, width), jnp.bfloat16),
            pltpu.SemaphoreType.DMA((count // block_rows(count),)),
        ],
        compiler_params=kernel_params(),
        cost_estimate=cost(count, width, scenarios),
    )(*operands)


def across_body(plane, count, sides, has_noise, has_terms, has_base, old_exact, new_exact, *refs):
    refs = list(refs)
    matrix_ref = refs.pop(0)
    noise_ref = refs.pop(0) if has_noise else None
    terms_refs = [refs.pop(0) for _ in sides] if has_terms else None
    base_ref = refs.pop(0) if has_base else None
    if old_exact:
        refs.pop(0)
    out_ref = refs.pop(0)
    exact_ref = refs.pop(0) if new_exact else None
    total_ref = refs.pop(0)
    streamed = plane is not None
    buffer_ref, sems = (refs.pop(0), refs.pop(0)) if streamed else (None, None)
    right_ref, right_sems = refs[:2] if has_noise else (None, None)
    exact_sems = refs[-1] if new_exact else None
    block = block_rows(count)
    blocks = count // block

    def first(part):
        return first_row(*sides[part], count)

    def noise_copy(part):
        return pltpu.make_async_copy(
            noise_ref.at[pl.ds(pl.multiple_of(first(part), count), count), :],
            right_ref.at[pl.ds(part * count, count), :],
            right_sems.at[part],
        )

    def exact_copy(part):
        return pltpu.make_async_copy(
            terms_refs[part],
            exact_ref.at[pl.ds(pl.multiple_of(first(part), count), count), :],
            exact_sems.at[part],
        )

    def matrix_copy(part, number):
        return block_copy(
            matrix_ref, plane, first(part), block, number, buffer_ref, part * count, sems, part * blocks
        )

    for part in range(len(sides)):
        if has_noise:
            noise_copy(part).start()
        for number in range(blocks if streamed else 0):
            matrix_copy(part, number).start()
    if new_exact:
        for part in range(len(sides)):
            exact_copy(part).start()
    if has_base:
        total_ref[...] = base_ref[...].T
    else:
        total_ref[...] = jnp.zeros_like(total_ref)
    for part in range(len(sides)):
        if has_noise:
            noise_copy(part).wait()

        def step(number, carry):
            if streamed:
                matrix_copy(part, number).wait()
            inner = pl.ds(pl.multiple_of(number * block, block), block)
            held = pl.ds(pl.multiple_of(part * count + number * block, block), block)
            if not has_noise:
                right = terms_refs[part][inner, :].astype(jnp.bfloat16)
            elif not has_terms:
                right = right_ref[held, :]
            else:
                right = right_ref[held, :].astype(jnp.float32) - terms_refs[part][inner, :]
                right = right.astype(jnp.bfloat16)
            if streamed:
                matrix = buffer_ref[held, :]
            else:
                matrix = matrix_ref[pl.ds(pl.multiple_of(first(part) + number * block, block), block), :]
            total_ref[...] += lax.dot_general(
                right, matrix, (((0,), (0,)), ((), ())), preferred_element_type=jnp.float32
            )
            return carry

        lax.fori_loop(0, blocks, step, 0)
    out_ref[...] = total_ref[...].T
    if new_exact:
        for part in range(len(sides)):
            exact_copy(part).wait()


def across_rows(matrix, plane, parts, count, noise=None, base=None, exact=None, give_exact=False):
    rows, width = matrix.shape[-2:]
    scenarios = (parts[0][0] if noise is None else noise).shape[1]
    sides = tuple((chunk, side) for _, chunk, side in parts)
    has_terms = parts[0][0] is not None
    streamed = plane is not None
    operands = [in_hbm(matrix) if streamed else in_vmem(matrix)]
    in_specs = [HBM if streamed else VMEM]
    if noise is not None:
        operands.append(in_hbm(noise))
        in_specs.append(HBM)
    if has_terms:
        operands += [in_vmem(terms) for terms, _, _ in parts]
        in_specs += [VMEM] * len(parts)
    if base is not None:
        operands.append(in_vmem(base))
        in_specs.append(VMEM)
    aliases = {}
    if exact is not None:
        operands.append(in_hbm(exact))
        in_specs.append(HBM)
        aliases = {len(operands) - 1: 1}
    out_shape = [pltpu.VMEM((width, scenarios), jnp.float32)]
    out_specs = [VMEM]
    held = len(parts) * count
    scratch = [pltpu.VMEM((scenarios, width), jnp.float32)]
    if streamed:
        scratch.append(pltpu.VMEM((held, width), jnp.bfloat16))
        scratch.append(pltpu.SemaphoreType.DMA((held // block_rows(count),)))
    if noise is not None:
        scratch += [pltpu.VMEM((held, scenarios), jnp.bfloat16), pltpu.SemaphoreType.DMA((len(parts),))]
    if give_exact:
        out_shape.append(pltpu.HBM((rows, scenarios), jnp.float32))
        out_specs.append(HBM)
        scratch.append(pltpu.SemaphoreType.DMA((len(parts),)))
    results = pl.pallas_call(
        functools.partial(
            across_body, plane, count, sides, noise is not None, has_terms, base is not None,
            exact is not None, give_exact,
        ),
        out_shape=tuple(out_shape),
        in_specs=in_specs,
        out_specs=tuple(out_specs),
        scratch_shapes=scratch,
        input_output_aliases=aliases,
        compiler_params=kernel_params(),
        cost_estimate=cost(held, width, scenarios),
    )(*operands)
    return tuple(results) if give_exact else results[0]


def load_body(plane, matrix_ref, ticket_ref, held_ref, out_ticket_ref, sems):
    copies = []
    block = block_rows(held_ref.shape[0])
    for number in range(held_ref.shape[0] // block):
        rows = pl.ds(number * block, block)
        copies.append(
            pltpu.make_async_copy(matrix_ref.at[plane, rows, :], held_ref.at[rows, :], sems.at[number])
        )
    for copy in copies:
        copy.start()
    out_ticket_ref[...] = ticket_ref[...]
    for copy in copies:
        copy.wait()


def load(matrix, plane, ticket):
    _, rows, width = matrix.shape
    return pl.pallas_call(
        functools.partial(load_body, plane),
        out_shape=(
            pltpu.VMEM((rows, width), matrix.dtype),
            pltpu.VMEM(ticket.shape, ticket.dtype),
        ),
        in_specs=[HBM, VMEM],
        out_specs=(VMEM, VMEM),
        scratch_shapes=[pltpu.SemaphoreType.DMA((rows // block_rows(rows),))],
        compiler_params=kernel_params(),
        cost_estimate=cost(rows, width, ticket.shape[1]),
    )(in_hbm(matrix), ticket)


def place_body(count, own_ref, other_ref, exact_ref, sems):
    copies = []
    for side, terms_ref in enumerate((own_ref, other_ref)):
        start = pl.multiple_of(first_row(0, side, count), count)
        copies.append(
            pltpu.make_async_copy(terms_ref, exact_ref.at[pl.ds(start, count), :], sems.at[side])
        )
    for copy in copies:
        copy.start()
    for copy in copies:
        copy.wait()


def place_rows(own, other):
    count, scenarios = own.shape
    return pl.pallas_call(
        functools.partial(place_body, count),
        out_shape=pltpu.HBM((2 * count, scenarios), jnp.float32),
        in_specs=[VMEM, VMEM],
        out_specs=HBM,
        scratch_shapes=[pltpu.SemaphoreType.DMA((2,))],
        compiler_params=kernel_params(),
    )(in_vmem(own), in_vmem(other))


def tied(first, second):
    return lax.optimization_barrier((first, second))


def run_jobs(jobs, inputs):
    return [job[1](given) for job, given in zip(jobs, inputs)]


def keep_results(jobs, results):
    for job, result in zip(jobs, results):
        job[2](result)


class Waits:
    def __init__(self):
        self.queue = []

    def put(self, *jobs):
        self.queue.append(list(jobs))

    def take(self):
        return self.queue.pop(0) if self.queue else []

    def drain(self):
        for jobs in self.queue:
            for job in jobs:
                job[2](job[1](job[0]()))
        self.queue = []


def exchanges(values, axis_positions, jobs=()):
    inputs = [job[0]() for job in jobs]
    values, inputs = tied(list(values), inputs)
    got = [swapped(value, axis, position) for value, (axis, position) in zip(values, axis_positions)]
    got, results = tied(got, run_jobs(jobs, inputs))
    keep_results(jobs, results)
    return values, got


def exchange(value, axis, position, jobs=()):
    values, got = exchanges([value], [(axis, position)], jobs)
    return values[0], got[0]


def halve(value, position, leaf_index, jobs):
    half_rows = value.shape[0] // 2
    upper = leaf_index >> position & 1
    kept = lax.dynamic_slice_in_dim(value, upper * half_rows, half_rows, 0)
    sent = lax.dynamic_slice_in_dim(value, (1 - upper) * half_rows, half_rows, 0)
    _, got = exchange(sent, "leaf", position, jobs)
    return kept + got


def double(value, position, leaf_index, jobs):
    value, partner = exchange(value, "leaf", position, jobs)
    upper = leaf_index >> position & 1
    return jnp.where(
        upper == 1,
        jnp.concatenate([partner, value], axis=0),
        jnp.concatenate([value, partner], axis=0),
    )


def group_sum(value, group_bits, leaf_index, waits):
    if group_bits == 0:
        return value
    if group_bits == 1:
        value, got = exchange(value, "leaf", 0, waits.take())
        return value + got
    if group_bits == 2:
        middle = value.shape[0] // 2
        parts = [value[:middle], value[middle:]]
        for positions in ((0, 1), (1, 0)):
            parts, got = exchanges(parts, [("leaf", position) for position in positions], waits.take())
            parts = [part + more for part, more in zip(parts, got)]
        return jnp.concatenate(parts, axis=0)
    for position in range(2):
        value = halve(value, position, leaf_index, waits.take())
    for position in range(2, group_bits):
        value, got = exchange(value, "leaf", position, waits.take())
        value = value + got
    for position in reversed(range(2)):
        value = double(value, position, leaf_index, waits.take())
    return value


def chunks_of(rows):
    return 2 if rows >= 4096 else 1


def rows_stage(produce, consume, chunks, waits):
    bits = bits_of("rows")
    owns = []
    for chunk in range(chunks):
        sent = produce(chunk, 1, owns[-1] if owns else None)
        kept = []
        job = (lambda: (), lambda _: produce(chunk, 0, sent), kept.append)
        _, got = exchange(sent, "rows", 0, [job])
        owns.append(kept[0] + got)
    gots = [swapped(own, "rows", 1) for own in owns]
    jobs = waits.take()
    owns[-1], inputs = tied(owns[-1], [job[0]() for job in jobs])
    gots[0], results = tied(gots[0], run_jobs(jobs, inputs))
    keep_results(jobs, results)
    state = None
    for chunk in range(chunks):
        got = gots[chunk]
        if chunk > 0:
            got, state = tied(got, state)
        own = owns[chunk] + got
        for position in range(2, bits):
            own = own + swapped(own, "rows", position)
        owns[chunk] = own
        if chunk + 1 < chunks:
            state = consume([(own, chunk, 0)], state)
    states = [state]
    job = (
        lambda: (owns[-1], state),
        lambda given: consume([(given[0], chunks - 1, 0)], given[1]),
        lambda result: states.append(result),
    )
    owns, others = exchanges(owns, [("rows", 0)] * chunks, [job])
    state = consume([(other, chunk, 1) for chunk, other in enumerate(others)], states[-1])
    parts = [(own, chunk, 0) for chunk, own in enumerate(owns)]
    parts += [(other, chunk, 1) for chunk, other in enumerate(others)]
    return state, parts


def on_device(
    factor_zero,
    factor_one,
    factor_two,
    factor_three,
    coupling_one,
    coupling_two,
    coupling_three,
    noise_zero,
    noise_one,
    noise_two,
    noise_three,
    tail_index,
):
    factors = [factor[None] for factor in (factor_zero, factor_one, factor_two, factor_three)]
    noises = [noise_zero, noise_one, noise_two, noise_three]
    couplings = {
        1: [jnp.transpose(coupling_one, (1, 0, 2))],
        2: [],
        3: [jnp.transpose(coupling_three, (1, 0, 2))],
    }
    leaf_bits = bits_of("leaf")
    leaf_index = lax.axis_index("leaf")
    width = factor_zero.shape[1]
    full_width = width * lax.axis_size("rows")
    scenario_count = noise_zero.shape[1]
    columns = jnp.arange(scenario_count, dtype=jnp.int32)
    counts = jnp.sum((tail_index[:, None] == columns[None, :]).astype(jnp.float32), axis=0)
    weights = 1.0 + counts

    early = {}
    held = {}
    tickets = [jnp.zeros((8, scenario_count), jnp.float32)]

    def load_job(name, plane):
        kind, level = name

        def run(given):
            matrix = factors[level] if kind == "factor" else couplings[level][0]
            held[name], out = load(matrix, plane, given)
            return out

        return (lambda: tickets[-1], run, tickets.append)

    def matrix_of(kind, level, plane):
        if (kind, level) in held:
            return held[kind, level], None
        return (factors[level] if kind == "factor" else couplings[level][0]), plane

    def turn_job():
        return (lambda: coupling_two, lambda given: jnp.transpose(given, (1, 0, 2)), couplings[2].append)

    def early_job(level, plane, vector):
        def run(given):
            return apply_rows(couplings[level][0], plane, given, early.get(level), 0, None, 1)

        return (lambda: vector, run, lambda result: early.__setitem__(level, result))

    def work(*steps):
        waits = Waits()
        for jobs in steps:
            waits.put(*jobs)
        return waits

    samples = []
    for tree_level in range(LEVELS):
        group_bits = leaf_bits - tree_level
        if tree_level == 0:
            part = across_rows(factors[0], 0, [(None, 0, None)], noise_zero.shape[0], noise=noise_zero)
        else:
            plane = tree_level - 1
            last = samples[-1].astype(jnp.bfloat16)
            if tree_level == 1:
                waits = work([turn_job()])
            elif tree_level == 2:
                waits = work([early_job(3, 1, last), load_job(("factor", 2), 0)])
            else:
                waits = work([load_job(("factor", 3), 0)])
            chunks = chunks_of(factors[tree_level].shape[1])

            def produce(chunk, side, after):
                vector = last
                if after is not None:
                    vector, _ = tied(vector, after)
                return apply_rows(
                    *matrix_of("coupling", tree_level, plane), vector, early.get(tree_level), chunk, side, chunks
                )

            factor = factors[tree_level]
            count = factor.shape[1] // chunks // 2

            def consume(parts, state):
                return across_rows(
                    *matrix_of("factor", tree_level, 0), parts, count, noise=noises[tree_level], base=state
                )

            part, _ = rows_stage(produce, consume, chunks, waits)
        if tree_level == 0:
            waits = work([], [], [], [], [load_job(("coupling", 1), 0), load_job(("factor", 1), 0)])
        elif tree_level == 1:
            waits = work(
                [early_job(3, 0, last)],
                [early_job(2, 0, last), load_job(("coupling", 2), 1)],
            )
        elif tree_level == 2:
            waits = work([load_job(("coupling", 3), 2)])
        else:
            waits = work()
        samples.append(group_sum(part, group_bits, leaf_index, waits))
        waits.drain()

    losses = []

    def loss_job(given):
        total = jnp.zeros((8, scenario_count), jnp.float32)
        for tree_level in range(LEVELS):
            group_bits = leaf_bits - tree_level
            piece_rows = given[tree_level].shape[0] >> group_bits
            member = leaf_index & (1 << group_bits) - 1
            own_rows = lax.dynamic_slice_in_dim(given[tree_level], member * piece_rows, piece_rows, 0)
            terms = weights[None, :] * jax.nn.softplus(own_rows - tail_level)
            total = total + jnp.sum(terms.reshape(-1, 8, scenario_count), axis=0)
        return total

    steps = [("leaf", position) for position in range(leaf_bits)]
    steps += [("rows", position) for position in range(bits_of("rows"))]

    def sum_job(count):
        def run(given):
            for _ in range(count):
                if steps:
                    axis, position = steps.pop(0)
                    given = given + swapped(given, axis, position)
            return given

        return (lambda: losses[-1], run, losses.append)

    pending = [None] * LEVELS
    gradients = [None] * LEVELS

    def later_job(level, plane):
        places = [(chunk, side) for _, chunk, side in solved[level]]

        def run(given):
            parts = [(terms, chunk, side) for terms, (chunk, side) in zip(given, places)]
            return across_rows(
                couplings[level][0], plane, parts, given[0].shape[0], base=pending[plane]
            )

        return (
            lambda: [terms for terms, _, _ in solved[level]],
            run,
            lambda result: pending.__setitem__(plane, result),
        )

    solved = {}
    for name in list(held):
        if name != ("factor", 3):
            del held[name]
    loss_start = (lambda: samples, loss_job, losses.append)
    for tree_level in reversed(range(LEVELS)):
        group_bits = leaf_bits - tree_level
        adjoint = weights[None, :] * jax.nn.sigmoid(samples[tree_level] - tail_level)
        if tree_level < LEVELS - 1:
            if tree_level == 2:
                waits = work(
                    [
                        later_job(3, 1), later_job(3, 0), load_job(("factor", 2), 0),
                    ]
                )
            elif tree_level == 1:
                waits = work(
                    [later_job(2, 0)], [load_job(("factor", 1), 0), sum_job(1)]
                )
            else:
                waits = work([sum_job(1)], [], [], [], [load_job(("factor", 0), 0)])
            adjoint = adjoint - group_sum(pending[tree_level], group_bits, leaf_index, waits)
            waits.drain()
        adjoint_round = adjoint.astype(jnp.bfloat16)
        chunks = chunks_of(factors[tree_level].shape[1])
        if tree_level == 3:
            waits = work([load_job(("coupling", 3), 2), loss_start])
        elif tree_level == 2:
            waits = work([load_job(("coupling", 2), 1), sum_job(2)])
        elif tree_level == 1:
            waits = work([load_job(("coupling", 1), 0), sum_job(1)])
        else:
            waits = work()

        def produce(chunk, side, after):
            vector = adjoint_round
            if after is not None:
                vector, _ = tied(vector, after)
            return apply_rows(*matrix_of("factor", tree_level, 0), vector, None, chunk, side, chunks)

        count = factors[tree_level].shape[1] // chunks // 2

        def consume(parts, state):
            if tree_level == 0:
                return ()
            base, exact = (None, None) if state is None else state
            return across_rows(
                *matrix_of("coupling", tree_level, tree_level - 1), parts, count,
                base=base, exact=exact, give_exact=True,
            )

        state, solved[tree_level] = rows_stage(produce, consume, chunks, waits)
        if tree_level == 0:
            gradients[0] = place_rows(*[terms for terms, _, _ in solved[0]])
            continue
        upward, gradients[tree_level] = state
        before = pending[tree_level - 1]
        pending[tree_level - 1] = upward if before is None else before + upward
    while steps:
        last_sum = sum_job(1)
        last_sum[2](last_sum[1](last_sum[0]()))
    tail_loss = jnp.sum(losses[-1] + tickets[-1]) / jnp.float32(
        (2**LEVELS - 1) * full_width * (scenario_count + tail_index.shape[0])
    )
    return (gradients[0], gradients[1], gradients[2], gradients[3], tail_loss)


def solution(mesh):
    in_specs = (
        P("leaf", "rows"),
        P("leaf", "rows"),
        P("leaf", "rows"),
        P("leaf", "rows"),
        P("leaf", None, "rows"),
        P("leaf", None, "rows"),
        P("leaf", None, "rows"),
        P("leaf", None),
        P("leaf", None),
        P("leaf", None),
        P("leaf", None),
        P(),
    )
    out_specs = (P("leaf", None), P("leaf", None), P("leaf", None), P("leaf", None), P())
    return jax.shard_map(
        on_device, mesh=mesh, in_specs=in_specs, out_specs=out_specs, check_vma=False
    )
```

```python
import functools

import jax
import jax.numpy as jnp
from jax import lax
from jax.experimental import pallas as pl
from jax.experimental.pallas import tpu as pltpu
from jax.sharding import PartitionSpec as P

LEVELS = 4


tail_level = 0.5


def swapped(x, axis, apart):
    return lax.ppermute(x, axis, [(i, i ^ 1 << apart) for i in range(lax.axis_size(axis))])


def bits_of(axis):
    return lax.axis_size(axis).bit_length() - 1


VMEM = pl.BlockSpec(memory_space=pltpu.VMEM)
HBM = pl.BlockSpec(memory_space=pltpu.HBM)


def in_hbm(array):
    return pltpu.with_memory_space_constraint(array, pltpu.HBM)


def in_vmem(array):
    return pltpu.with_memory_space_constraint(array, pltpu.VMEM)


def kernel_params():
    return pltpu.CompilerParams(vmem_limit_bytes=14 * 1024 * 1024)


def cost(rows, width, scenarios):
    return pl.CostEstimate(flops=scenarios, transcendentals=0, bytes_accessed=scenarios)


def block_rows(rows):
    return min(rows, max(128, rows // 4))


def first_row(chunk, side, count):
    if side is None:
        return chunk * count
    low = lax.axis_index("rows") & 1
    return (2 * chunk + (low if side == 0 else 1 - low)) * count


def block_copy(matrix_ref, plane, first, block, number, buffer_ref, base, sems, sem_base):
    start = pl.multiple_of(first + number * block, block)
    place = pl.multiple_of(base + number * block, block)
    return pltpu.make_async_copy(
        matrix_ref.at[plane, pl.ds(start, block), :],
        buffer_ref.at[pl.ds(place, block), :],
        sems.at[sem_base + number],
    )


def apply_body(plane, chunk, side, count, has_base, matrix_ref, vector_ref, *refs):
    start = first_row(chunk, side, count)
    if plane is None:
        rows = pl.ds(pl.multiple_of(start, count), count)
        product = jnp.dot(matrix_ref[rows, :], vector_ref[...], preferred_element_type=jnp.float32)
        if has_base:
            product = product + refs[0][rows, :]
        refs[-1][...] = product
        return
    out_ref, buffer_ref, sems = refs[-3:]
    block = block_rows(count)
    blocks = count // block
    for number in range(blocks):
        block_copy(matrix_ref, plane, start, block, number, buffer_ref, 0, sems, 0).start()

    def step(number, carry):
        block_copy(matrix_ref, plane, start, block, number, buffer_ref, 0, sems, 0).wait()
        rows = pl.ds(pl.multiple_of(number * block, block), block)
        product = jnp.dot(buffer_ref[rows, :], vector_ref[...], preferred_element_type=jnp.float32)
        if has_base:
            product = product + refs[0][pl.ds(pl.multiple_of(start + number * block, block), block), :]
        out_ref[rows, :] = product
        return carry

    lax.fori_loop(0, blocks, step, 0)


def apply_rows(matrix, plane, vector, base, chunk, side, chunks):
    rows, width = matrix.shape[-2:]
    count = rows // chunks if side is None else rows // chunks // 2
    scenarios = vector.shape[1]
    held = plane is None
    operands = [in_vmem(matrix) if held else in_hbm(matrix), in_vmem(vector)]
    operands += [] if base is None else [in_vmem(base)]
    return pl.pallas_call(
        functools.partial(apply_body, plane, chunk, side, count, base is not None),
        out_shape=pltpu.VMEM((count, scenarios), jnp.float32),
        in_specs=[VMEM if held else HBM] + [VMEM] * (len(operands) - 1),
        out_specs=VMEM,
        scratch_shapes=[]
        if held
        else [
            pltpu.VMEM((count, width), jnp.bfloat16),
            pltpu.SemaphoreType.DMA((count // block_rows(count),)),
        ],
        compiler_params=kernel_params(),
        cost_estimate=cost(count, width, scenarios),
    )(*operands)


def across_body(plane, count, sides, noise_held, has_terms, has_base, has_extra, old_exact, new_exact, final, *refs):
    refs = list(refs)
    has_noise = noise_held is not None
    matrix_ref = refs.pop(0)
    noise_ref = refs.pop(0) if has_noise else None
    terms_refs = [refs.pop(0) for _ in sides] if has_terms else None
    base_ref = refs.pop(0) if has_base else None
    extra_ref = refs.pop(0) if has_extra else None
    if old_exact:
        refs.pop(0)
    out_ref = refs.pop(0)
    exact_ref = refs.pop(0) if new_exact else None
    total_ref = refs.pop(0)
    streamed = plane is not None
    buffer_ref, sems = (refs.pop(0), refs.pop(0)) if streamed else (None, None)
    right_ref, right_sems = refs[:2] if noise_held is False else (None, None)
    exact_sems = refs[-1] if new_exact else None
    block = block_rows(count)
    blocks = count // block

    def first(part):
        return first_row(*sides[part], count)

    def noise_copy(part):
        return pltpu.make_async_copy(
            noise_ref.at[pl.ds(pl.multiple_of(first(part), count), count), :],
            right_ref.at[pl.ds(part * count, count), :],
            right_sems.at[part],
        )

    def exact_copy(part):
        return pltpu.make_async_copy(
            terms_refs[part],
            exact_ref.at[pl.ds(pl.multiple_of(first(part), count), count), :],
            exact_sems.at[part],
        )

    def matrix_copy(part, number):
        return block_copy(
            matrix_ref, plane, first(part), block, number, buffer_ref, part * count, sems, part * blocks
        )

    for part in range(len(sides)):
        if noise_held is False:
            noise_copy(part).start()
        for number in range(blocks if streamed else 0):
            matrix_copy(part, number).start()
    if new_exact:
        for part in range(len(sides)):
            exact_copy(part).start()
    if has_base:
        total_ref[...] = base_ref[...]
    else:
        total_ref[...] = jnp.zeros_like(total_ref)
    for part in range(len(sides)):
        if noise_held is False:
            noise_copy(part).wait()

        def step(number, carry):
            if streamed:
                matrix_copy(part, number).wait()
            inner = pl.ds(pl.multiple_of(number * block, block), block)
            held = pl.ds(pl.multiple_of(part * count + number * block, block), block)
            place = pl.ds(pl.multiple_of(first(part) + number * block, block), block)
            if noise_held:
                noise = noise_ref[place, :]
            elif has_noise:
                noise = right_ref[held, :]
            if not has_noise:
                right = terms_refs[part][inner, :].astype(jnp.bfloat16)
            elif not has_terms:
                right = noise
            else:
                right = (noise.astype(jnp.float32) - terms_refs[part][inner, :]).astype(jnp.bfloat16)
            if streamed:
                matrix = buffer_ref[held, :]
            else:
                matrix = matrix_ref[place, :]
            total_ref[...] += lax.dot_general(
                right, matrix, (((0,), (0,)), ((), ())), preferred_element_type=jnp.float32
            )
            return carry

        lax.fori_loop(0, blocks, step, 0)
    total = total_ref[...].T if final else total_ref[...]
    out_ref[...] = total + extra_ref[...] if has_extra else total
    if new_exact:
        for part in range(len(sides)):
            exact_copy(part).wait()


def across_rows(
    matrix, plane, parts, count, noise=None, noise_held=None, base=None, extra=None, exact=None,
    give_exact=False, final=True,
):
    rows, width = matrix.shape[-2:]
    scenarios = (parts[0][0] if noise is None else noise).shape[1]
    sides = tuple((chunk, side) for _, chunk, side in parts)
    has_terms = parts[0][0] is not None
    streamed = plane is not None
    operands = [in_hbm(matrix) if streamed else in_vmem(matrix)]
    in_specs = [HBM if streamed else VMEM]
    if noise is not None:
        operands.append(in_vmem(noise) if noise_held else in_hbm(noise))
        in_specs.append(VMEM if noise_held else HBM)
    if has_terms:
        operands += [in_vmem(terms) for terms, _, _ in parts]
        in_specs += [VMEM] * len(parts)
    if base is not None:
        operands.append(in_vmem(base))
        in_specs.append(VMEM)
    if extra is not None:
        operands.append(in_vmem(extra))
        in_specs.append(VMEM)
    aliases = {}
    if exact is not None:
        operands.append(in_hbm(exact))
        in_specs.append(HBM)
        aliases = {len(operands) - 1: 1}
    out_shape = [pltpu.VMEM((width, scenarios) if final else (scenarios, width), jnp.float32)]
    out_specs = [VMEM]
    held = len(parts) * count
    scratch = [pltpu.VMEM((scenarios, width), jnp.float32)]
    if streamed:
        scratch.append(pltpu.VMEM((held, width), jnp.bfloat16))
        scratch.append(pltpu.SemaphoreType.DMA((held // block_rows(count),)))
    if noise_held is False:
        scratch += [pltpu.VMEM((held, scenarios), jnp.bfloat16), pltpu.SemaphoreType.DMA((len(parts),))]
    if give_exact:
        out_shape.append(pltpu.HBM((rows, scenarios), jnp.float32))
        out_specs.append(HBM)
        scratch.append(pltpu.SemaphoreType.DMA((len(parts),)))
    results = pl.pallas_call(
        functools.partial(
            across_body, plane, count, sides, noise_held, has_terms, base is not None,
            extra is not None, exact is not None, give_exact, final,
        ),
        out_shape=tuple(out_shape),
        in_specs=in_specs,
        out_specs=tuple(out_specs),
        scratch_shapes=scratch,
        input_output_aliases=aliases,
        compiler_params=kernel_params(),
        cost_estimate=cost(held, width, scenarios),
    )(*operands)
    return tuple(results) if give_exact else results[0]


def load_body(plane, has_noise, matrix_ref, ticket_ref, *refs):
    refs = list(refs)
    noise_ref = refs.pop(0) if has_noise else None
    held_ref, out_ticket_ref = refs[:2]
    sems = refs[-1]
    copies = []
    if has_noise:
        copies.append(pltpu.make_async_copy(noise_ref, refs[2], sems.at[sems.shape[0] - 1]))
    block = block_rows(held_ref.shape[0])
    for number in range(held_ref.shape[0] // block):
        rows = pl.ds(number * block, block)
        copies.append(
            pltpu.make_async_copy(matrix_ref.at[plane, rows, :], held_ref.at[rows, :], sems.at[number])
        )
    for copy in copies:
        copy.start()
    out_ticket_ref[...] = ticket_ref[...]
    for copy in copies:
        copy.wait()


def load(matrix, plane, ticket, noise):
    _, rows, width = matrix.shape
    operands = [in_hbm(matrix), ticket]
    out_shape = [pltpu.VMEM((rows, width), matrix.dtype), pltpu.VMEM(ticket.shape, ticket.dtype)]
    if noise is not None:
        operands.append(in_hbm(noise))
        out_shape.append(pltpu.VMEM(noise.shape, noise.dtype))
    return pl.pallas_call(
        functools.partial(load_body, plane, noise is not None),
        out_shape=tuple(out_shape),
        in_specs=[HBM, VMEM] + [HBM] * (len(operands) - 2),
        out_specs=(VMEM,) * len(out_shape),
        scratch_shapes=[pltpu.SemaphoreType.DMA((rows // block_rows(rows) + 1,))],
        compiler_params=kernel_params(),
        cost_estimate=cost(rows, width, ticket.shape[1]),
    )(*operands)


def place_body(count, own_ref, other_ref, exact_ref, sems):
    copies = []
    for side, terms_ref in enumerate((own_ref, other_ref)):
        start = pl.multiple_of(first_row(0, side, count), count)
        copies.append(
            pltpu.make_async_copy(terms_ref, exact_ref.at[pl.ds(start, count), :], sems.at[side])
        )
    for copy in copies:
        copy.start()
    for copy in copies:
        copy.wait()


def place_rows(own, other):
    count, scenarios = own.shape
    return pl.pallas_call(
        functools.partial(place_body, count),
        out_shape=pltpu.HBM((2 * count, scenarios), jnp.float32),
        in_specs=[VMEM, VMEM],
        out_specs=HBM,
        scratch_shapes=[pltpu.SemaphoreType.DMA((2,))],
        compiler_params=kernel_params(),
    )(in_vmem(own), in_vmem(other))


def tied(first, second):
    return lax.optimization_barrier((first, second))


def run_jobs(jobs, inputs):
    return [job[1](given) for job, given in zip(jobs, inputs)]


def keep_results(jobs, results):
    for job, result in zip(jobs, results):
        job[2](result)


class Waits:
    def __init__(self):
        self.queue = []

    def put(self, *jobs):
        self.queue.append(list(jobs))

    def take(self):
        return self.queue.pop(0) if self.queue else []

    def drain(self):
        for jobs in self.queue:
            for job in jobs:
                job[2](job[1](job[0]()))
        self.queue = []


def exchanges(values, axis_positions, jobs=()):
    inputs = [job[0]() for job in jobs]
    values, inputs = tied(list(values), inputs)
    got = [swapped(value, axis, position) for value, (axis, position) in zip(values, axis_positions)]
    got, results = tied(got, run_jobs(jobs, inputs))
    keep_results(jobs, results)
    return values, got


def exchange(value, axis, position, jobs=()):
    values, got = exchanges([value], [(axis, position)], jobs)
    return values[0], got[0]


def halves_at(value, position, leaf_index):
    half_rows = value.shape[0] // 2
    upper = leaf_index >> position & 1
    kept = lax.dynamic_slice_in_dim(value, upper * half_rows, half_rows, 0)
    sent = lax.dynamic_slice_in_dim(value, (1 - upper) * half_rows, half_rows, 0)
    return kept, sent


def joined_at(value, partner, position, leaf_index):
    upper = leaf_index >> position & 1
    return jnp.where(
        upper == 1,
        jnp.concatenate([partner, value], axis=0),
        jnp.concatenate([value, partner], axis=0),
    )


def group_sum(value, group_bits, leaf_index, waits):
    if group_bits == 0:
        return value
    if group_bits == 1:
        value, got = exchange(value, "leaf", 0, waits.take())
        return value + got
    if group_bits == 2:
        middle = value.shape[0] // 2
        parts = [value[:middle], value[middle:]]
        for positions in ((0, 1), (1, 0)):
            parts, got = exchanges(parts, [("leaf", position) for position in positions], waits.take())
            parts = [part + more for part, more in zip(parts, got)]
        return jnp.concatenate(parts, axis=0)
    middle = value.shape[0] // 2
    parts = [value[:middle], value[middle:]]
    for positions in ((0, 1), (1, 0)):
        pairs = [halves_at(part, position, leaf_index) for part, position in zip(parts, positions)]
        _, got = exchanges(
            [sent for _, sent in pairs], [("leaf", position) for position in positions], waits.take()
        )
        parts = [kept + more for (kept, _), more in zip(pairs, got)]
    value = jnp.concatenate(parts, axis=0)
    for position in range(2, group_bits):
        value, got = exchange(value, "leaf", position, waits.take())
        value = value + got
    middle = value.shape[0] // 2
    parts = [value[:middle], value[middle:]]
    for positions in ((1, 0), (0, 1)):
        parts, got = exchanges(parts, [("leaf", position) for position in positions], waits.take())
        parts = [
            joined_at(part, more, position, leaf_index)
            for part, more, position in zip(parts, got, positions)
        ]
    return jnp.concatenate(parts, axis=0)


def chunks_of(rows):
    return 2 if rows >= 4096 else 1


def rows_stage(produce, consume, chunks, waits):
    bits = bits_of("rows")
    owns = []
    for chunk in range(chunks):
        sent = produce(chunk, 1, owns[-1] if owns else None)
        kept = []
        job = (lambda: (), lambda _: produce(chunk, 0, sent), kept.append)
        _, got = exchange(sent, "rows", 0, [job])
        owns.append(kept[0] + got)
    gots = [swapped(own, "rows", 1) for own in owns]
    jobs = waits.take()
    owns[-1], inputs = tied(owns[-1], [job[0]() for job in jobs])
    gots[0], results = tied(gots[0], run_jobs(jobs, inputs))
    keep_results(jobs, results)
    state = None
    for chunk in range(chunks):
        got = gots[chunk]
        if chunk > 0:
            got, state = tied(got, state)
        own = owns[chunk] + got
        for position in range(2, bits):
            own = own + swapped(own, "rows", position)
        owns[chunk] = own
        if chunk + 1 < chunks:
            state = consume([(own, chunk, 0)], state, False)
    states = [state]
    job = (
        lambda: (owns[-1], state),
        lambda given: consume([(given[0], chunks - 1, 0)], given[1], False),
        lambda result: states.append(result),
    )
    owns, others = exchanges(owns, [("rows", 0)] * chunks, [job])
    state = consume([(other, chunk, 1) for chunk, other in enumerate(others)], states[-1], True)
    parts = [(own, chunk, 0) for chunk, own in enumerate(owns)]
    parts += [(other, chunk, 1) for chunk, other in enumerate(others)]
    return state, parts


def on_device(
    factor_zero,
    factor_one,
    factor_two,
    factor_three,
    coupling_one,
    coupling_two,
    coupling_three,
    noise_zero,
    noise_one,
    noise_two,
    noise_three,
    tail_index,
):
    factors = [factor[None] for factor in (factor_zero, factor_one, factor_two, factor_three)]
    noises = [noise_zero, noise_one, noise_two, noise_three]
    couplings = {
        1: [jnp.transpose(coupling_one, (1, 0, 2))],
        2: [],
        3: [jnp.transpose(coupling_three, (1, 0, 2))],
    }
    leaf_bits = bits_of("leaf")
    leaf_index = lax.axis_index("leaf")
    width = factor_zero.shape[1]
    full_width = width * lax.axis_size("rows")
    scenario_count = noise_zero.shape[1]
    columns = jnp.arange(scenario_count, dtype=jnp.int32)
    counts = jnp.sum((tail_index[:, None] == columns[None, :]).astype(jnp.float32), axis=0)
    weights = 1.0 + counts

    early = {}
    held = {}
    tickets = [jnp.zeros((8, scenario_count), jnp.float32)]

    def load_job(name, plane, forward=False):
        kind, level = name

        def run(given):
            matrix = factors[level] if kind == "factor" else couplings[level][0]
            noise = noises[level] if kind == "factor" and forward else None
            held[name], out, *rest = load(matrix, plane, given, noise)
            if rest:
                held["noise", level] = rest[0]
            return out

        return (lambda: tickets[-1], run, tickets.append)

    def matrix_of(kind, level, plane):
        if (kind, level) in held:
            return held[kind, level], None
        return (factors[level] if kind == "factor" else couplings[level][0]), plane

    def turn_job():
        return (lambda: coupling_two, lambda given: jnp.transpose(given, (1, 0, 2)), couplings[2].append)

    def early_job(level, plane, vector):
        def run(given):
            return apply_rows(couplings[level][0], plane, given, early.get(level), 0, None, 1)

        return (lambda: vector, run, lambda result: early.__setitem__(level, result))

    def work(*steps):
        waits = Waits()
        for jobs in steps:
            waits.put(*jobs)
        return waits

    samples = []
    for tree_level in range(LEVELS):
        group_bits = leaf_bits - tree_level
        if tree_level == 0:
            part = across_rows(factors[0], 0, [(None, 0, None)], noise_zero.shape[0], noise=noise_zero, noise_held=False)
        else:
            plane = tree_level - 1
            last = samples[-1].astype(jnp.bfloat16)
            if tree_level == 1:
                waits = work([turn_job()])
            elif tree_level == 2:
                waits = work([early_job(3, 1, last), load_job(("factor", 2), 0, True)])
            else:
                waits = work([load_job(("factor", 3), 0, True)])
            chunks = chunks_of(factors[tree_level].shape[1])

            def produce(chunk, side, after):
                vector = last
                if after is not None:
                    vector, _ = tied(vector, after)
                return apply_rows(
                    *matrix_of("coupling", tree_level, plane), vector, early.get(tree_level), chunk, side, chunks
                )

            factor = factors[tree_level]
            count = factor.shape[1] // chunks // 2

            def consume(parts, state, final):
                noise_held = ("noise", tree_level) in held
                noise = held["noise", tree_level] if noise_held else noises[tree_level]
                return across_rows(
                    *matrix_of("factor", tree_level, 0), parts, count, noise=noise, noise_held=noise_held,
                    base=state, final=final,
                )

            part, _ = rows_stage(produce, consume, chunks, waits)
        if tree_level == 0:
            waits = work([], [], [], [], [load_job(("coupling", 1), 0), load_job(("factor", 1), 0, True)])
        elif tree_level == 1:
            waits = work(
                [early_job(3, 0, last)],
                [early_job(2, 0, last), load_job(("coupling", 2), 1)],
            )
        elif tree_level == 2:
            waits = work([load_job(("coupling", 3), 2)])
        else:
            waits = work()
        samples.append(group_sum(part, group_bits, leaf_index, waits))
        waits.drain()

    losses = []

    def loss_job(given):
        total = jnp.zeros((8, scenario_count), jnp.float32)
        for tree_level in range(LEVELS):
            group_bits = leaf_bits - tree_level
            piece_rows = given[tree_level].shape[0] >> group_bits
            member = leaf_index & (1 << group_bits) - 1
            own_rows = lax.dynamic_slice_in_dim(given[tree_level], member * piece_rows, piece_rows, 0)
            terms = weights[None, :] * jax.nn.softplus(own_rows - tail_level)
            total = total + jnp.sum(terms.reshape(-1, 8, scenario_count), axis=0)
        return total

    steps = [("leaf", position) for position in range(leaf_bits)]
    steps += [("rows", position) for position in range(bits_of("rows"))]

    def sum_job(count):
        def run(given):
            for _ in range(count):
                if steps:
                    axis, position = steps.pop(0)
                    given = given + swapped(given, axis, position)
            return given

        return (lambda: losses[-1], run, losses.append)

    pending = [None] * LEVELS
    gradients = [None] * LEVELS

    def later_job(level, plane):
        places = [(chunk, side) for _, chunk, side in solved[level]]

        def run(given):
            parts = [(terms, chunk, side) for terms, (chunk, side) in zip(given, places)]
            return across_rows(
                couplings[level][0], plane, parts, given[0].shape[0], extra=pending[plane]
            )

        return (
            lambda: [terms for terms, _, _ in solved[level]],
            run,
            lambda result: pending.__setitem__(plane, result),
        )

    solved = {}
    for name in list(held):
        if name != ("factor", 3):
            del held[name]
    loss_start = (lambda: samples, loss_job, losses.append)
    for tree_level in reversed(range(LEVELS)):
        group_bits = leaf_bits - tree_level
        adjoint = weights[None, :] * jax.nn.sigmoid(samples[tree_level] - tail_level)
        if tree_level < LEVELS - 1:
            if tree_level == 2:
                waits = work(
                    [
                        later_job(3, 1), later_job(3, 0), load_job(("factor", 2), 0),
                    ]
                )
            elif tree_level == 1:
                waits = work(
                    [later_job(2, 0)], [load_job(("factor", 1), 0), sum_job(1)]
                )
            else:
                waits = work([sum_job(1)], [], [], [], [load_job(("factor", 0), 0)])
            adjoint = adjoint - group_sum(pending[tree_level], group_bits, leaf_index, waits)
            waits.drain()
        adjoint_round = adjoint.astype(jnp.bfloat16)
        chunks = chunks_of(factors[tree_level].shape[1])
        if tree_level == 3:
            waits = work([load_job(("coupling", 3), 2), loss_start])
        elif tree_level == 2:
            waits = work([load_job(("coupling", 2), 1), sum_job(2)])
        elif tree_level == 1:
            waits = work([load_job(("coupling", 1), 0), sum_job(1)])
        else:
            waits = work()

        def produce(chunk, side, after):
            vector = adjoint_round
            if after is not None:
                vector, _ = tied(vector, after)
            place = matrix_of("factor", tree_level, 0)
            if chunk > 0 and side == 0:
                place = (factors[tree_level], 0)
            return apply_rows(*place, vector, None, chunk, side, chunks)

        count = factors[tree_level].shape[1] // chunks // 2

        def consume(parts, state, final):
            if tree_level == 0:
                return ()
            base, exact = (None, None) if state is None else state
            return across_rows(
                *matrix_of("coupling", tree_level, tree_level - 1), parts, count,
                base=base, extra=pending[tree_level - 1] if final else None, exact=exact, give_exact=True,
                final=final,
            )

        state, solved[tree_level] = rows_stage(produce, consume, chunks, waits)
        if tree_level == 0:
            gradients[0] = place_rows(*[terms for terms, _, _ in solved[0]])
            continue
        pending[tree_level - 1], gradients[tree_level] = state
    while steps:
        last_sum = sum_job(1)
        last_sum[2](last_sum[1](last_sum[0]()))
    tail_loss = jnp.sum(losses[-1] + tickets[-1]) / jnp.float32(
        (2**LEVELS - 1) * full_width * (scenario_count + tail_index.shape[0])
    )
    return (gradients[0], gradients[1], gradients[2], gradients[3], tail_loss)


def solution(mesh):
    in_specs = (
        P("leaf", "rows"),
        P("leaf", "rows"),
        P("leaf", "rows"),
        P("leaf", "rows"),
        P("leaf", None, "rows"),
        P("leaf", None, "rows"),
        P("leaf", None, "rows"),
        P("leaf", None),
        P("leaf", None),
        P("leaf", None),
        P("leaf", None),
        P(),
    )
    out_specs = (P("leaf", None), P("leaf", None), P("leaf", None), P("leaf", None), P())
    return jax.shard_map(
        on_device, mesh=mesh, in_specs=in_specs, out_specs=out_specs, check_vma=False
    )
```

```python
import functools

import jax
import jax.numpy as jnp
from jax import lax
from jax.experimental import pallas as pl
from jax.experimental.pallas import tpu as pltpu
from jax.sharding import PartitionSpec as P

LEVELS = 4


tail_level = 0.5


def moved(x, axis, flips):
    return lax.ppermute(x, axis, [(i, i ^ flips) for i in range(lax.axis_size(axis))])


def swapped(x, axis, apart):
    return moved(x, axis, 1 << apart)


def bits_of(axis):
    return lax.axis_size(axis).bit_length() - 1


VMEM = pl.BlockSpec(memory_space=pltpu.VMEM)
HBM = pl.BlockSpec(memory_space=pltpu.HBM)


def in_hbm(array):
    return pltpu.with_memory_space_constraint(array, pltpu.HBM)


def in_vmem(array):
    return pltpu.with_memory_space_constraint(array, pltpu.VMEM)


def kernel_params():
    return pltpu.CompilerParams(vmem_limit_bytes=14 * 1024 * 1024)


def cost(rows, width, scenarios):
    return pl.CostEstimate(flops=scenarios, transcendentals=0, bytes_accessed=scenarios)


def block_rows(rows):
    return min(rows, max(128, rows // 4))


def first_row(chunk, side, count):
    if side is None:
        return chunk * count
    low = lax.axis_index("rows") & 1
    return (2 * chunk + (low if side == 0 else 1 - low)) * count


def block_copy(matrix_ref, plane, first, block, number, buffer_ref, base, sems, sem_base):
    start = pl.multiple_of(first + number * block, block)
    place = pl.multiple_of(base + number * block, block)
    return pltpu.make_async_copy(
        matrix_ref.at[plane, pl.ds(start, block), :],
        buffer_ref.at[pl.ds(place, block), :],
        sems.at[sem_base + number],
    )


def apply_body(plane, chunk, side, count, has_base, matrix_ref, vector_ref, *refs):
    start = first_row(chunk, side, count)
    if plane is None:
        rows = pl.ds(pl.multiple_of(start, count), count)
        product = jnp.dot(matrix_ref[rows, :], vector_ref[...], preferred_element_type=jnp.float32)
        if has_base:
            product = product + refs[0][rows, :]
        refs[-1][...] = product
        return
    out_ref, buffer_ref, sems = refs[-3:]
    block = block_rows(count)
    blocks = count // block
    for number in range(blocks):
        block_copy(matrix_ref, plane, start, block, number, buffer_ref, 0, sems, 0).start()

    def step(number, carry):
        block_copy(matrix_ref, plane, start, block, number, buffer_ref, 0, sems, 0).wait()
        rows = pl.ds(pl.multiple_of(number * block, block), block)
        product = jnp.dot(buffer_ref[rows, :], vector_ref[...], preferred_element_type=jnp.float32)
        if has_base:
            product = product + refs[0][pl.ds(pl.multiple_of(start + number * block, block), block), :]
        out_ref[rows, :] = product
        return carry

    lax.fori_loop(0, blocks, step, 0)


def apply_rows(matrix, plane, vector, base, chunk, side, chunks):
    rows, width = matrix.shape[-2:]
    count = rows // chunks if side is None else rows // chunks // 2
    scenarios = vector.shape[1]
    held = plane is None
    operands = [in_vmem(matrix) if held else in_hbm(matrix), in_vmem(vector)]
    operands += [] if base is None else [in_vmem(base)]
    return pl.pallas_call(
        functools.partial(apply_body, plane, chunk, side, count, base is not None),
        out_shape=pltpu.VMEM((count, scenarios), jnp.float32),
        in_specs=[VMEM if held else HBM] + [VMEM] * (len(operands) - 1),
        out_specs=VMEM,
        scratch_shapes=[]
        if held
        else [
            pltpu.VMEM((count, width), jnp.bfloat16),
            pltpu.SemaphoreType.DMA((count // block_rows(count),)),
        ],
        compiler_params=kernel_params(),
        cost_estimate=cost(count, width, scenarios),
    )(*operands)


def across_body(plane, count, sides, noise_held, has_terms, has_base, has_extra, old_exact, new_exact, final, *refs):
    refs = list(refs)
    has_noise = noise_held is not None
    matrix_ref = refs.pop(0)
    noise_ref = refs.pop(0) if has_noise else None
    terms_refs = [refs.pop(0) for _ in sides] if has_terms else None
    base_ref = refs.pop(0) if has_base else None
    extra_ref = refs.pop(0) if has_extra else None
    if old_exact:
        refs.pop(0)
    out_ref = refs.pop(0)
    exact_ref = refs.pop(0) if new_exact else None
    total_ref = refs.pop(0)
    streamed = plane is not None
    buffer_ref, sems = (refs.pop(0), refs.pop(0)) if streamed else (None, None)
    right_ref, right_sems = refs[:2] if noise_held is False else (None, None)
    exact_sems = refs[-1] if new_exact else None
    block = block_rows(count)
    blocks = count // block

    def first(part):
        return first_row(*sides[part], count)

    def noise_copy(part):
        return pltpu.make_async_copy(
            noise_ref.at[pl.ds(pl.multiple_of(first(part), count), count), :],
            right_ref.at[pl.ds(part * count, count), :],
            right_sems.at[part],
        )

    def exact_copy(part):
        return pltpu.make_async_copy(
            terms_refs[part],
            exact_ref.at[pl.ds(pl.multiple_of(first(part), count), count), :],
            exact_sems.at[part],
        )

    def matrix_copy(part, number):
        return block_copy(
            matrix_ref, plane, first(part), block, number, buffer_ref, part * count, sems, part * blocks
        )

    for part in range(len(sides)):
        if noise_held is False:
            noise_copy(part).start()
        for number in range(blocks if streamed else 0):
            matrix_copy(part, number).start()
    if new_exact:
        for part in range(len(sides)):
            exact_copy(part).start()
    if has_base:
        total_ref[...] = base_ref[...]
    else:
        total_ref[...] = jnp.zeros_like(total_ref)
    for part in range(len(sides)):
        if noise_held is False:
            noise_copy(part).wait()

        def step(number, carry):
            if streamed:
                matrix_copy(part, number).wait()
            inner = pl.ds(pl.multiple_of(number * block, block), block)
            held = pl.ds(pl.multiple_of(part * count + number * block, block), block)
            place = pl.ds(pl.multiple_of(first(part) + number * block, block), block)
            if noise_held:
                noise = noise_ref[place, :]
            elif has_noise:
                noise = right_ref[held, :]
            if not has_noise:
                right = terms_refs[part][inner, :].astype(jnp.bfloat16)
            elif not has_terms:
                right = noise
            else:
                right = (noise.astype(jnp.float32) - terms_refs[part][inner, :]).astype(jnp.bfloat16)
            if streamed:
                matrix = buffer_ref[held, :]
            else:
                matrix = matrix_ref[place, :]
            total_ref[...] += lax.dot_general(
                right, matrix, (((0,), (0,)), ((), ())), preferred_element_type=jnp.float32
            )
            return carry

        lax.fori_loop(0, blocks, step, 0)
    total = total_ref[...].T if final else total_ref[...]
    out_ref[...] = total + extra_ref[...] if has_extra else total
    if new_exact:
        for part in range(len(sides)):
            exact_copy(part).wait()


def across_rows(
    matrix, plane, parts, count, noise=None, noise_held=None, base=None, extra=None, exact=None,
    give_exact=False, final=True,
):
    rows, width = matrix.shape[-2:]
    scenarios = (parts[0][0] if noise is None else noise).shape[1]
    sides = tuple((chunk, side) for _, chunk, side in parts)
    has_terms = parts[0][0] is not None
    streamed = plane is not None
    operands = [in_hbm(matrix) if streamed else in_vmem(matrix)]
    in_specs = [HBM if streamed else VMEM]
    if noise is not None:
        operands.append(in_vmem(noise) if noise_held else in_hbm(noise))
        in_specs.append(VMEM if noise_held else HBM)
    if has_terms:
        operands += [in_vmem(terms) for terms, _, _ in parts]
        in_specs += [VMEM] * len(parts)
    if base is not None:
        operands.append(in_vmem(base))
        in_specs.append(VMEM)
    if extra is not None:
        operands.append(in_vmem(extra))
        in_specs.append(VMEM)
    aliases = {}
    if exact is not None:
        operands.append(in_hbm(exact))
        in_specs.append(HBM)
        aliases = {len(operands) - 1: 1}
    out_shape = [pltpu.VMEM((width, scenarios) if final else (scenarios, width), jnp.float32)]
    out_specs = [VMEM]
    held = len(parts) * count
    scratch = [pltpu.VMEM((scenarios, width), jnp.float32)]
    if streamed:
        scratch.append(pltpu.VMEM((held, width), jnp.bfloat16))
        scratch.append(pltpu.SemaphoreType.DMA((held // block_rows(count),)))
    if noise_held is False:
        scratch += [pltpu.VMEM((held, scenarios), jnp.bfloat16), pltpu.SemaphoreType.DMA((len(parts),))]
    if give_exact:
        out_shape.append(pltpu.HBM((rows, scenarios), jnp.float32))
        out_specs.append(HBM)
        scratch.append(pltpu.SemaphoreType.DMA((len(parts),)))
    results = pl.pallas_call(
        functools.partial(
            across_body, plane, count, sides, noise_held, has_terms, base is not None,
            extra is not None, exact is not None, give_exact, final,
        ),
        out_shape=tuple(out_shape),
        in_specs=in_specs,
        out_specs=tuple(out_specs),
        scratch_shapes=scratch,
        input_output_aliases=aliases,
        compiler_params=kernel_params(),
        cost_estimate=cost(held, width, scenarios),
    )(*operands)
    return tuple(results) if give_exact else results[0]


def load_body(plane, has_noise, matrix_ref, ticket_ref, *refs):
    refs = list(refs)
    noise_ref = refs.pop(0) if has_noise else None
    held_ref, out_ticket_ref = refs[:2]
    sems = refs[-1]
    copies = []
    if has_noise:
        copies.append(pltpu.make_async_copy(noise_ref, refs[2], sems.at[sems.shape[0] - 1]))
    block = block_rows(held_ref.shape[0])
    for number in range(held_ref.shape[0] // block):
        rows = pl.ds(number * block, block)
        copies.append(
            pltpu.make_async_copy(matrix_ref.at[plane, rows, :], held_ref.at[rows, :], sems.at[number])
        )
    for copy in copies:
        copy.start()
    out_ticket_ref[...] = ticket_ref[...]
    for copy in copies:
        copy.wait()


def load(matrix, plane, ticket, noise):
    _, rows, width = matrix.shape
    operands = [in_hbm(matrix), ticket]
    out_shape = [pltpu.VMEM((rows, width), matrix.dtype), pltpu.VMEM(ticket.shape, ticket.dtype)]
    if noise is not None:
        operands.append(in_hbm(noise))
        out_shape.append(pltpu.VMEM(noise.shape, noise.dtype))
    return pl.pallas_call(
        functools.partial(load_body, plane, noise is not None),
        out_shape=tuple(out_shape),
        in_specs=[HBM, VMEM] + [HBM] * (len(operands) - 2),
        out_specs=(VMEM,) * len(out_shape),
        scratch_shapes=[pltpu.SemaphoreType.DMA((rows // block_rows(rows) + 1,))],
        compiler_params=kernel_params(),
        cost_estimate=cost(rows, width, ticket.shape[1]),
    )(*operands)


def place_body(count, own_ref, other_ref, exact_ref, sems):
    copies = []
    for side, terms_ref in enumerate((own_ref, other_ref)):
        start = pl.multiple_of(first_row(0, side, count), count)
        copies.append(
            pltpu.make_async_copy(terms_ref, exact_ref.at[pl.ds(start, count), :], sems.at[side])
        )
    for copy in copies:
        copy.start()
    for copy in copies:
        copy.wait()


def place_rows(own, other):
    count, scenarios = own.shape
    return pl.pallas_call(
        functools.partial(place_body, count),
        out_shape=pltpu.HBM((2 * count, scenarios), jnp.float32),
        in_specs=[VMEM, VMEM],
        out_specs=HBM,
        scratch_shapes=[pltpu.SemaphoreType.DMA((2,))],
        compiler_params=kernel_params(),
    )(in_vmem(own), in_vmem(other))


def tied(first, second):
    return lax.optimization_barrier((first, second))


def run_jobs(jobs, inputs):
    return [job[1](given) for job, given in zip(jobs, inputs)]


def keep_results(jobs, results):
    for job, result in zip(jobs, results):
        job[2](result)


class Waits:
    def __init__(self):
        self.queue = []

    def put(self, *jobs):
        self.queue.append(list(jobs))

    def take(self):
        return self.queue.pop(0) if self.queue else []

    def drain(self):
        for jobs in self.queue:
            for job in jobs:
                job[2](job[1](job[0]()))
        self.queue = []


def exchanges(values, axis_flips, jobs=()):
    inputs = [job[0]() for job in jobs]
    values, inputs = tied(list(values), inputs)
    got = [moved(value, axis, flips) for value, (axis, flips) in zip(values, axis_flips)]
    got, results = tied(got, run_jobs(jobs, inputs))
    keep_results(jobs, results)
    return values, got


def exchange(value, axis, position, jobs=()):
    values, got = exchanges([value], [(axis, 1 << position)], jobs)
    return values[0], got[0]


def joined_at(value, partner, position, leaf_index):
    upper = leaf_index >> position & 1
    return jnp.where(
        upper == 1,
        jnp.concatenate([partner, value], axis=0),
        jnp.concatenate([value, partner], axis=0),
    )


def group_sum(value, group_bits, leaf_index, waits):
    if group_bits == 0:
        return value
    if group_bits == 1:
        value, got = exchange(value, "leaf", 0, waits.take())
        return value + got
    if group_bits == 2:
        middle = value.shape[0] // 2
        parts = [value[:middle], value[middle:]]
        for positions in ((0, 1), (1, 0)):
            parts, got = exchanges(parts, [("leaf", 1 << position) for position in positions], waits.take())
            parts = [part + more for part, more in zip(parts, got)]
        return jnp.concatenate(parts, axis=0)
    quarter = value.shape[0] // 4
    member = leaf_index & 3
    pieces = [
        lax.dynamic_slice_in_dim(value, (member ^ flips) * quarter, quarter, 0) for flips in range(4)
    ]
    routes = [("leaf", flips) for flips in (1, 2, 3)]
    _, got = exchanges(pieces[1:], routes, waits.take())
    value = (pieces[0] + got[0]) + (got[1] + got[2])
    for position in range(2, group_bits):
        value, got = exchange(value, "leaf", position, waits.take())
        value = value + got
    values, got = exchanges([value] * 3, routes, waits.take())
    near = joined_at(values[0], got[0], 0, leaf_index)
    far = joined_at(got[1], got[2], 0, leaf_index)
    return joined_at(near, far, 1, leaf_index)


def chunks_of(rows):
    return 2 if rows >= 4096 else 1


def rows_stage(produce, consume, chunks, waits):
    bits = bits_of("rows")
    owns = []
    for chunk in range(chunks):
        sent = produce(chunk, 1, owns[-1] if owns else None)
        kept = []
        job = (lambda: (), lambda _: produce(chunk, 0, sent), kept.append)
        _, got = exchange(sent, "rows", 0, [job])
        owns.append(kept[0] + got)
    gots = [swapped(own, "rows", 1) for own in owns]
    jobs = waits.take()
    owns[-1], inputs = tied(owns[-1], [job[0]() for job in jobs])
    gots[0], results = tied(gots[0], run_jobs(jobs, inputs))
    keep_results(jobs, results)
    state = None
    for chunk in range(chunks):
        got = gots[chunk]
        if chunk > 0:
            got, state = tied(got, state)
        own = owns[chunk] + got
        for position in range(2, bits):
            own = own + swapped(own, "rows", position)
        owns[chunk] = own
        if chunk + 1 < chunks:
            state = consume([(own, chunk, 0)], state, False)
    states = [state]
    job = (
        lambda: (owns[-1], state),
        lambda given: consume([(given[0], chunks - 1, 0)], given[1], False),
        lambda result: states.append(result),
    )
    owns, others = exchanges(owns, [("rows", 1)] * chunks, [job])
    state = consume([(other, chunk, 1) for chunk, other in enumerate(others)], states[-1], True)
    parts = [(own, chunk, 0) for chunk, own in enumerate(owns)]
    parts += [(other, chunk, 1) for chunk, other in enumerate(others)]
    return state, parts


def on_device(
    factor_zero,
    factor_one,
    factor_two,
    factor_three,
    coupling_one,
    coupling_two,
    coupling_three,
    noise_zero,
    noise_one,
    noise_two,
    noise_three,
    tail_index,
):
    factors = [factor[None] for factor in (factor_zero, factor_one, factor_two, factor_three)]
    noises = [noise_zero, noise_one, noise_two, noise_three]
    couplings = {
        1: [jnp.transpose(coupling_one, (1, 0, 2))],
        2: [],
        3: [jnp.transpose(coupling_three, (1, 0, 2))],
    }
    leaf_bits = bits_of("leaf")
    leaf_index = lax.axis_index("leaf")
    width = factor_zero.shape[1]
    full_width = width * lax.axis_size("rows")
    scenario_count = noise_zero.shape[1]
    columns = jnp.arange(scenario_count, dtype=jnp.int32)
    counts = jnp.sum((tail_index[:, None] == columns[None, :]).astype(jnp.float32), axis=0)
    weights = 1.0 + counts

    early = {}
    held = {}
    tickets = [jnp.zeros((8, scenario_count), jnp.float32)]

    def load_job(name, plane, forward=False):
        kind, level = name

        def run(given):
            matrix = factors[level] if kind == "factor" else couplings[level][0]
            noise = noises[level] if kind == "factor" and forward else None
            held[name], out, *rest = load(matrix, plane, given, noise)
            if rest:
                held["noise", level] = rest[0]
            return out

        return (lambda: tickets[-1], run, tickets.append)

    def matrix_of(kind, level, plane):
        if (kind, level) in held:
            return held[kind, level], None
        return (factors[level] if kind == "factor" else couplings[level][0]), plane

    def turn_job():
        return (lambda: coupling_two, lambda given: jnp.transpose(given, (1, 0, 2)), couplings[2].append)

    def early_job(level, plane, vector):
        def run(given):
            return apply_rows(couplings[level][0], plane, given, early.get(level), 0, None, 1)

        return (lambda: vector, run, lambda result: early.__setitem__(level, result))

    def work(*steps):
        waits = Waits()
        for jobs in steps:
            waits.put(*jobs)
        return waits

    samples = []
    for tree_level in range(LEVELS):
        group_bits = leaf_bits - tree_level
        if tree_level == 0:
            part = across_rows(factors[0], 0, [(None, 0, None)], noise_zero.shape[0], noise=noise_zero, noise_held=False)
        else:
            plane = tree_level - 1
            last = samples[-1].astype(jnp.bfloat16)
            if tree_level == 1:
                waits = work([turn_job()])
            elif tree_level == 2:
                waits = work([early_job(3, 1, last), load_job(("factor", 2), 0, True)])
            else:
                waits = work([load_job(("factor", 3), 0, True)])
            chunks = chunks_of(factors[tree_level].shape[1])

            def produce(chunk, side, after):
                vector = last
                if after is not None:
                    vector, _ = tied(vector, after)
                return apply_rows(
                    *matrix_of("coupling", tree_level, plane), vector, early.get(tree_level), chunk, side, chunks
                )

            factor = factors[tree_level]
            count = factor.shape[1] // chunks // 2

            def consume(parts, state, final):
                noise_held = ("noise", tree_level) in held
                noise = held["noise", tree_level] if noise_held else noises[tree_level]
                return across_rows(
                    *matrix_of("factor", tree_level, 0), parts, count, noise=noise, noise_held=noise_held,
                    base=state, final=final,
                )

            part, _ = rows_stage(produce, consume, chunks, waits)
        if tree_level == 0:
            waits = work([], [], [load_job(("coupling", 1), 0), load_job(("factor", 1), 0, True)])
        elif tree_level == 1:
            waits = work(
                [early_job(3, 0, last)],
                [early_job(2, 0, last), load_job(("coupling", 2), 1)],
            )
        elif tree_level == 2:
            waits = work([load_job(("coupling", 3), 2)])
        else:
            waits = work()
        samples.append(group_sum(part, group_bits, leaf_index, waits))
        waits.drain()

    losses = []

    def loss_job(given):
        total = jnp.zeros((8, scenario_count), jnp.float32)
        for tree_level in range(LEVELS):
            group_bits = leaf_bits - tree_level
            piece_rows = given[tree_level].shape[0] >> group_bits
            member = leaf_index & (1 << group_bits) - 1
            own_rows = lax.dynamic_slice_in_dim(given[tree_level], member * piece_rows, piece_rows, 0)
            terms = weights[None, :] * jax.nn.softplus(own_rows - tail_level)
            total = total + jnp.sum(terms.reshape(-1, 8, scenario_count), axis=0)
        return total

    steps = [("leaf", position) for position in range(leaf_bits)]
    steps += [("rows", position) for position in range(bits_of("rows"))]

    def sum_job(count):
        def run(given):
            for _ in range(count):
                if steps:
                    axis, position = steps.pop(0)
                    given = given + swapped(given, axis, position)
            return given

        return (lambda: losses[-1], run, losses.append)

    pending = [None] * LEVELS
    gradients = [None] * LEVELS

    def later_job(level, plane):
        places = [(chunk, side) for _, chunk, side in solved[level]]

        def run(given):
            parts = [(terms, chunk, side) for terms, (chunk, side) in zip(given, places)]
            return across_rows(
                couplings[level][0], plane, parts, given[0].shape[0], extra=pending[plane]
            )

        return (
            lambda: [terms for terms, _, _ in solved[level]],
            run,
            lambda result: pending.__setitem__(plane, result),
        )

    solved = {}
    for name in list(held):
        if name != ("factor", 3):
            del held[name]
    loss_start = (lambda: samples, loss_job, losses.append)
    for tree_level in reversed(range(LEVELS)):
        group_bits = leaf_bits - tree_level
        adjoint = weights[None, :] * jax.nn.sigmoid(samples[tree_level] - tail_level)
        if tree_level < LEVELS - 1:
            if tree_level == 2:
                waits = work(
                    [
                        later_job(3, 1), later_job(3, 0), load_job(("factor", 2), 0),
                    ]
                )
            elif tree_level == 1:
                waits = work(
                    [later_job(2, 0)], [load_job(("factor", 1), 0), sum_job(1)]
                )
            else:
                waits = work([sum_job(1)], [], [load_job(("factor", 0), 0)])
            adjoint = adjoint - group_sum(pending[tree_level], group_bits, leaf_index, waits)
            waits.drain()
        adjoint_round = adjoint.astype(jnp.bfloat16)
        chunks = chunks_of(factors[tree_level].shape[1])
        if tree_level == 3:
            waits = work([load_job(("coupling", 3), 2), loss_start])
        elif tree_level == 2:
            waits = work([load_job(("coupling", 2), 1), sum_job(2)])
        elif tree_level == 1:
            waits = work([load_job(("coupling", 1), 0), sum_job(1)])
        else:
            waits = work()

        def produce(chunk, side, after):
            vector = adjoint_round
            if after is not None:
                vector, _ = tied(vector, after)
            place = matrix_of("factor", tree_level, 0)
            if chunk > 0 and side == 0:
                place = (factors[tree_level], 0)
            return apply_rows(*place, vector, None, chunk, side, chunks)

        count = factors[tree_level].shape[1] // chunks // 2

        def consume(parts, state, final):
            if tree_level == 0:
                return ()
            base, exact = (None, None) if state is None else state
            return across_rows(
                *matrix_of("coupling", tree_level, tree_level - 1), parts, count,
                base=base, extra=pending[tree_level - 1] if final else None, exact=exact, give_exact=True,
                final=final,
            )

        state, solved[tree_level] = rows_stage(produce, consume, chunks, waits)
        if tree_level == 0:
            gradients[0] = place_rows(*[terms for terms, _, _ in solved[0]])
            continue
        pending[tree_level - 1], gradients[tree_level] = state
    while steps:
        last_sum = sum_job(1)
        last_sum[2](last_sum[1](last_sum[0]()))
    tail_loss = jnp.sum(losses[-1] + tickets[-1]) / jnp.float32(
        (2**LEVELS - 1) * full_width * (scenario_count + tail_index.shape[0])
    )
    return (gradients[0], gradients[1], gradients[2], gradients[3], tail_loss)


def solution(mesh):
    in_specs = (
        P("leaf", "rows"),
        P("leaf", "rows"),
        P("leaf", "rows"),
        P("leaf", "rows"),
        P("leaf", None, "rows"),
        P("leaf", None, "rows"),
        P("leaf", None, "rows"),
        P("leaf", None),
        P("leaf", None),
        P("leaf", None),
        P("leaf", None),
        P(),
    )
    out_specs = (P("leaf", None), P("leaf", None), P("leaf", None), P("leaf", None), P())
    return jax.shard_map(
        on_device, mesh=mesh, in_specs=in_specs, out_specs=out_specs, check_vma=False
    )
```

```python
import functools

import jax
import jax.numpy as jnp
from jax import lax
from jax.experimental import pallas as pl
from jax.experimental.pallas import tpu as pltpu
from jax.sharding import PartitionSpec as P

LEVELS = 4


tail_level = 0.5


def moved(x, axis, flips):
    return lax.ppermute(x, axis, [(i, i ^ flips) for i in range(lax.axis_size(axis))])


def swapped(x, axis, apart):
    return moved(x, axis, 1 << apart)


def bits_of(axis):
    return lax.axis_size(axis).bit_length() - 1


VMEM = pl.BlockSpec(memory_space=pltpu.VMEM)
HBM = pl.BlockSpec(memory_space=pltpu.HBM)


def in_hbm(array):
    return pltpu.with_memory_space_constraint(array, pltpu.HBM)


def in_vmem(array):
    return pltpu.with_memory_space_constraint(array, pltpu.VMEM)


def kernel_params():
    return pltpu.CompilerParams(vmem_limit_bytes=14 * 1024 * 1024)


def cost(rows, width, scenarios):
    return pl.CostEstimate(flops=scenarios, transcendentals=0, bytes_accessed=scenarios)


def block_rows(rows):
    return min(rows, max(128, rows // 4))


def first_row(chunk, side, count):
    if side is None:
        return chunk * count
    low = lax.axis_index("rows") & 1
    return (2 * chunk + (low if side == 0 else 1 - low)) * count


def block_copy(matrix_ref, plane, first, block, number, buffer_ref, base, sems, sem_base):
    start = pl.multiple_of(first + number * block, block)
    place = pl.multiple_of(base + number * block, block)
    return pltpu.make_async_copy(
        matrix_ref.at[plane, pl.ds(start, block), :],
        buffer_ref.at[pl.ds(place, block), :],
        sems.at[sem_base + number],
    )


def apply_body(plane, chunk, side, count, has_base, matrix_ref, vector_ref, *refs):
    start = first_row(chunk, side, count)
    if plane is None:
        rows = pl.ds(pl.multiple_of(start, count), count)
        product = jnp.dot(matrix_ref[rows, :], vector_ref[...], preferred_element_type=jnp.float32)
        if has_base:
            product = product + refs[0][rows, :]
        refs[-1][...] = product
        return
    out_ref, buffer_ref, sems = refs[-3:]
    block = block_rows(count)
    blocks = count // block
    for number in range(blocks):
        block_copy(matrix_ref, plane, start, block, number, buffer_ref, 0, sems, 0).start()

    def step(number, carry):
        block_copy(matrix_ref, plane, start, block, number, buffer_ref, 0, sems, 0).wait()
        rows = pl.ds(pl.multiple_of(number * block, block), block)
        product = jnp.dot(buffer_ref[rows, :], vector_ref[...], preferred_element_type=jnp.float32)
        if has_base:
            product = product + refs[0][pl.ds(pl.multiple_of(start + number * block, block), block), :]
        out_ref[rows, :] = product
        return carry

    lax.fori_loop(0, blocks, step, 0)


def apply_rows(matrix, plane, vector, base, chunk, side, chunks):
    rows, width = matrix.shape[-2:]
    count = rows // chunks if side is None else rows // chunks // 2
    scenarios = vector.shape[1]
    held = plane is None
    operands = [in_vmem(matrix) if held else in_hbm(matrix), in_vmem(vector)]
    operands += [] if base is None else [in_vmem(base)]
    return pl.pallas_call(
        functools.partial(apply_body, plane, chunk, side, count, base is not None),
        out_shape=pltpu.VMEM((count, scenarios), jnp.float32),
        in_specs=[VMEM if held else HBM] + [VMEM] * (len(operands) - 1),
        out_specs=VMEM,
        scratch_shapes=[]
        if held
        else [
            pltpu.VMEM((count, width), jnp.bfloat16),
            pltpu.SemaphoreType.DMA((count // block_rows(count),)),
        ],
        compiler_params=kernel_params(),
        cost_estimate=cost(count, width, scenarios),
    )(*operands)


def across_body(plane, count, sides, noise_held, has_terms, has_base, has_extra, old_exact, new_exact, final, *refs):
    refs = list(refs)
    has_noise = noise_held is not None
    matrix_ref = refs.pop(0)
    noise_ref = refs.pop(0) if has_noise else None
    terms_refs = [refs.pop(0) for _ in sides] if has_terms else None
    base_ref = refs.pop(0) if has_base else None
    extra_ref = refs.pop(0) if has_extra else None
    if old_exact:
        refs.pop(0)
    out_ref = refs.pop(0)
    exact_ref = refs.pop(0) if new_exact else None
    total_ref = refs.pop(0)
    streamed = plane is not None
    buffer_ref, sems = (refs.pop(0), refs.pop(0)) if streamed else (None, None)
    right_ref, right_sems = refs[:2] if noise_held is False else (None, None)
    exact_sems = refs[-1] if new_exact else None
    block = block_rows(count)
    blocks = count // block

    def first(part):
        return first_row(*sides[part], count)

    def noise_copy(part):
        return pltpu.make_async_copy(
            noise_ref.at[pl.ds(pl.multiple_of(first(part), count), count), :],
            right_ref.at[pl.ds(part * count, count), :],
            right_sems.at[part],
        )

    def exact_copy(part):
        return pltpu.make_async_copy(
            terms_refs[part],
            exact_ref.at[pl.ds(pl.multiple_of(first(part), count), count), :],
            exact_sems.at[part],
        )

    def matrix_copy(part, number):
        return block_copy(
            matrix_ref, plane, first(part), block, number, buffer_ref, part * count, sems, part * blocks
        )

    for part in range(len(sides)):
        if noise_held is False:
            noise_copy(part).start()
        for number in range(blocks if streamed else 0):
            matrix_copy(part, number).start()
    if new_exact:
        for part in range(len(sides)):
            exact_copy(part).start()
    if has_base:
        total_ref[...] = base_ref[...]
    else:
        total_ref[...] = jnp.zeros_like(total_ref)
    for part in range(len(sides)):
        if noise_held is False:
            noise_copy(part).wait()

        def step(number, carry):
            if streamed:
                matrix_copy(part, number).wait()
            inner = pl.ds(pl.multiple_of(number * block, block), block)
            held = pl.ds(pl.multiple_of(part * count + number * block, block), block)
            place = pl.ds(pl.multiple_of(first(part) + number * block, block), block)
            if noise_held:
                noise = noise_ref[place, :]
            elif has_noise:
                noise = right_ref[held, :]
            if not has_noise:
                right = terms_refs[part][inner, :].astype(jnp.bfloat16)
            elif not has_terms:
                right = noise
            else:
                right = (noise.astype(jnp.float32) - terms_refs[part][inner, :]).astype(jnp.bfloat16)
            if streamed:
                matrix = buffer_ref[held, :]
            else:
                matrix = matrix_ref[place, :]
            total_ref[...] += lax.dot_general(
                right, matrix, (((0,), (0,)), ((), ())), preferred_element_type=jnp.float32
            )
            return carry

        lax.fori_loop(0, blocks, step, 0)
    total = total_ref[...].T if final else total_ref[...]
    out_ref[...] = total + extra_ref[...] if has_extra else total
    if new_exact:
        for part in range(len(sides)):
            exact_copy(part).wait()


def across_rows(
    matrix, plane, parts, count, noise=None, noise_held=None, base=None, extra=None, exact=None,
    give_exact=False, final=True,
):
    rows, width = matrix.shape[-2:]
    scenarios = (parts[0][0] if noise is None else noise).shape[1]
    sides = tuple((chunk, side) for _, chunk, side in parts)
    has_terms = parts[0][0] is not None
    streamed = plane is not None
    operands = [in_hbm(matrix) if streamed else in_vmem(matrix)]
    in_specs = [HBM if streamed else VMEM]
    if noise is not None:
        operands.append(in_vmem(noise) if noise_held else in_hbm(noise))
        in_specs.append(VMEM if noise_held else HBM)
    if has_terms:
        operands += [in_vmem(terms) for terms, _, _ in parts]
        in_specs += [VMEM] * len(parts)
    if base is not None:
        operands.append(in_vmem(base))
        in_specs.append(VMEM)
    if extra is not None:
        operands.append(in_vmem(extra))
        in_specs.append(VMEM)
    aliases = {}
    if exact is not None:
        operands.append(in_hbm(exact))
        in_specs.append(HBM)
        aliases = {len(operands) - 1: 1}
    out_shape = [pltpu.VMEM((width, scenarios) if final else (scenarios, width), jnp.float32)]
    out_specs = [VMEM]
    held = len(parts) * count
    scratch = [pltpu.VMEM((scenarios, width), jnp.float32)]
    if streamed:
        scratch.append(pltpu.VMEM((held, width), jnp.bfloat16))
        scratch.append(pltpu.SemaphoreType.DMA((held // block_rows(count),)))
    if noise_held is False:
        scratch += [pltpu.VMEM((held, scenarios), jnp.bfloat16), pltpu.SemaphoreType.DMA((len(parts),))]
    if give_exact:
        out_shape.append(pltpu.HBM((rows, scenarios), jnp.float32))
        out_specs.append(HBM)
        scratch.append(pltpu.SemaphoreType.DMA((len(parts),)))
    results = pl.pallas_call(
        functools.partial(
            across_body, plane, count, sides, noise_held, has_terms, base is not None,
            extra is not None, exact is not None, give_exact, final,
        ),
        out_shape=tuple(out_shape),
        in_specs=in_specs,
        out_specs=tuple(out_specs),
        scratch_shapes=scratch,
        input_output_aliases=aliases,
        compiler_params=kernel_params(),
        cost_estimate=cost(held, width, scenarios),
    )(*operands)
    return tuple(results) if give_exact else results[0]


def load_body(plane, has_noise, matrix_ref, ticket_ref, *refs):
    refs = list(refs)
    noise_ref = refs.pop(0) if has_noise else None
    held_ref, out_ticket_ref = refs[:2]
    sems = refs[-1]
    copies = []
    if has_noise:
        copies.append(pltpu.make_async_copy(noise_ref, refs[2], sems.at[sems.shape[0] - 1]))
    block = block_rows(held_ref.shape[0])
    for number in range(held_ref.shape[0] // block):
        rows = pl.ds(number * block, block)
        copies.append(
            pltpu.make_async_copy(matrix_ref.at[plane, rows, :], held_ref.at[rows, :], sems.at[number])
        )
    for copy in copies:
        copy.start()
    out_ticket_ref[...] = ticket_ref[...]
    for copy in copies:
        copy.wait()


def load(matrix, plane, ticket, noise):
    _, rows, width = matrix.shape
    operands = [in_hbm(matrix), ticket]
    out_shape = [pltpu.VMEM((rows, width), matrix.dtype), pltpu.VMEM(ticket.shape, ticket.dtype)]
    if noise is not None:
        operands.append(in_hbm(noise))
        out_shape.append(pltpu.VMEM(noise.shape, noise.dtype))
    return pl.pallas_call(
        functools.partial(load_body, plane, noise is not None),
        out_shape=tuple(out_shape),
        in_specs=[HBM, VMEM] + [HBM] * (len(operands) - 2),
        out_specs=(VMEM,) * len(out_shape),
        scratch_shapes=[pltpu.SemaphoreType.DMA((rows // block_rows(rows) + 1,))],
        compiler_params=kernel_params(),
        cost_estimate=cost(rows, width, ticket.shape[1]),
    )(*operands)


def place_body(count, own_ref, other_ref, exact_ref, sems):
    copies = []
    for side, terms_ref in enumerate((own_ref, other_ref)):
        start = pl.multiple_of(first_row(0, side, count), count)
        copies.append(
            pltpu.make_async_copy(terms_ref, exact_ref.at[pl.ds(start, count), :], sems.at[side])
        )
    for copy in copies:
        copy.start()
    for copy in copies:
        copy.wait()


def place_rows(own, other):
    count, scenarios = own.shape
    return pl.pallas_call(
        functools.partial(place_body, count),
        out_shape=pltpu.HBM((2 * count, scenarios), jnp.float32),
        in_specs=[VMEM, VMEM],
        out_specs=HBM,
        scratch_shapes=[pltpu.SemaphoreType.DMA((2,))],
        compiler_params=kernel_params(),
    )(in_vmem(own), in_vmem(other))


def tied(first, second):
    return lax.optimization_barrier((first, second))


def run_jobs(jobs, inputs):
    return [job[1](given) for job, given in zip(jobs, inputs)]


def keep_results(jobs, results):
    for job, result in zip(jobs, results):
        job[2](result)


class Waits:
    def __init__(self):
        self.queue = []

    def put(self, *jobs):
        self.queue.append(list(jobs))

    def take(self):
        return self.queue.pop(0) if self.queue else []

    def drain(self):
        for jobs in self.queue:
            for job in jobs:
                job[2](job[1](job[0]()))
        self.queue = []


def exchanges(values, axis_flips, jobs=()):
    inputs = [job[0]() for job in jobs]
    values, inputs = tied(list(values), inputs)
    got = [moved(value, axis, flips) for value, (axis, flips) in zip(values, axis_flips)]
    got, results = tied(got, run_jobs(jobs, inputs))
    keep_results(jobs, results)
    return values, got


def exchange(value, axis, position, jobs=()):
    values, got = exchanges([value], [(axis, 1 << position)], jobs)
    return values[0], got[0]


def joined_at(value, partner, position, leaf_index):
    upper = leaf_index >> position & 1
    return jnp.where(
        upper == 1,
        jnp.concatenate([partner, value], axis=0),
        jnp.concatenate([value, partner], axis=0),
    )


def group_sum(value, group_bits, leaf_index, waits):
    if group_bits == 0:
        return value
    if group_bits == 1:
        value, got = exchange(value, "leaf", 0, waits.take())
        return value + got
    if group_bits == 2:
        middle = value.shape[0] // 2
        parts = [value[:middle], value[middle:]]
        for positions in ((0, 1), (1, 0)):
            parts, got = exchanges(parts, [("leaf", 1 << position) for position in positions], waits.take())
            parts = [part + more for part, more in zip(parts, got)]
        return jnp.concatenate(parts, axis=0)
    quarter = value.shape[0] // 4
    member = leaf_index & 3
    pieces = [
        lax.dynamic_slice_in_dim(value, (member ^ flips) * quarter, quarter, 0) for flips in range(4)
    ]
    routes = [("leaf", flips) for flips in (1, 2, 3)]
    _, got = exchanges(pieces[1:], routes, waits.take())
    value = (pieces[0] + got[0]) + (got[1] + got[2])
    for position in range(2, group_bits):
        value, got = exchange(value, "leaf", position, waits.take())
        value = value + got
    values, got = exchanges([value] * 3, routes, waits.take())
    near = joined_at(values[0], got[0], 0, leaf_index)
    far = joined_at(got[1], got[2], 0, leaf_index)
    return joined_at(near, far, 1, leaf_index)


def chunks_of(rows):
    return 2 if rows >= 4096 else 1


def rows_stage(produce, consume, chunks, waits, ahead):
    bits = bits_of("rows")
    owns = []
    sents = [produce(0, 1, None)]
    for chunk in range(chunks):
        if len(sents) == chunk:
            sents.append(produce(chunk, 1, owns[-1]))
        sent = sents[chunk]
        kept = []

        def beneath(_):
            parts = [produce(chunk, 0, sent)]
            if ahead and chunk + 1 < chunks:
                parts.append(produce(chunk + 1, 1, sent))
            return parts

        _, got = exchange(sent, "rows", 0, [(lambda: (), beneath, kept.extend)])
        owns.append(kept[0] + got)
        sents += kept[1:]
    gots = [swapped(own, "rows", 1) for own in owns]
    jobs = waits.take()
    owns[-1], inputs = tied(owns[-1], [job[0]() for job in jobs])
    gots[0], results = tied(gots[0], run_jobs(jobs, inputs))
    keep_results(jobs, results)
    state = None
    for chunk in range(chunks):
        got = gots[chunk]
        if chunk > 0:
            got, state = tied(got, state)
        own = owns[chunk] + got
        for position in range(2, bits):
            own = own + swapped(own, "rows", position)
        owns[chunk] = own
        if chunk + 1 < chunks:
            state = consume([(own, chunk, 0)], state, False)
    states = [state]
    job = (
        lambda: (owns[-1], state),
        lambda given: consume([(given[0], chunks - 1, 0)], given[1], False),
        lambda result: states.append(result),
    )
    owns, others = exchanges(owns, [("rows", 1)] * chunks, [job])
    state = consume([(other, chunk, 1) for chunk, other in enumerate(others)], states[-1], True)
    parts = [(own, chunk, 0) for chunk, own in enumerate(owns)]
    parts += [(other, chunk, 1) for chunk, other in enumerate(others)]
    return state, parts


def on_device(
    factor_zero,
    factor_one,
    factor_two,
    factor_three,
    coupling_one,
    coupling_two,
    coupling_three,
    noise_zero,
    noise_one,
    noise_two,
    noise_three,
    tail_index,
):
    factors = [factor[None] for factor in (factor_zero, factor_one, factor_two, factor_three)]
    noises = [noise_zero, noise_one, noise_two, noise_three]
    couplings = {
        1: [jnp.transpose(coupling_one, (1, 0, 2))],
        2: [],
        3: [jnp.transpose(coupling_three, (1, 0, 2))],
    }
    leaf_bits = bits_of("leaf")
    leaf_index = lax.axis_index("leaf")
    width = factor_zero.shape[1]
    full_width = width * lax.axis_size("rows")
    scenario_count = noise_zero.shape[1]
    columns = jnp.arange(scenario_count, dtype=jnp.int32)
    counts = jnp.sum((tail_index[:, None] == columns[None, :]).astype(jnp.float32), axis=0)
    weights = 1.0 + counts

    early = {}
    held = {}
    tickets = [jnp.zeros((8, scenario_count), jnp.float32)]

    def load_job(name, plane, forward=False):
        kind, level = name

        def run(given):
            matrix = factors[level] if kind == "factor" else couplings[level][0]
            noise = noises[level] if kind == "factor" and forward else None
            held[name], out, *rest = load(matrix, plane, given, noise)
            if rest:
                held["noise", level] = rest[0]
            return out

        return (lambda: tickets[-1], run, tickets.append)

    def matrix_of(kind, level, plane):
        if (kind, level) in held:
            return held[kind, level], None
        return (factors[level] if kind == "factor" else couplings[level][0]), plane

    def turn_job():
        return (lambda: coupling_two, lambda given: jnp.transpose(given, (1, 0, 2)), couplings[2].append)

    def early_job(level, plane, vector):
        def run(given):
            return apply_rows(couplings[level][0], plane, given, early.get(level), 0, None, 1)

        return (lambda: vector, run, lambda result: early.__setitem__(level, result))

    def work(*steps):
        waits = Waits()
        for jobs in steps:
            waits.put(*jobs)
        return waits

    samples = []
    for tree_level in range(LEVELS):
        group_bits = leaf_bits - tree_level
        if tree_level == 0:
            part = across_rows(factors[0], 0, [(None, 0, None)], noise_zero.shape[0], noise=noise_zero, noise_held=False)
        else:
            plane = tree_level - 1
            last = samples[-1].astype(jnp.bfloat16)
            if tree_level == 1:
                waits = work([turn_job()])
            elif tree_level == 2:
                waits = work([early_job(3, 1, last), load_job(("factor", 2), 0, True)])
            else:
                waits = work([load_job(("factor", 3), 0, True)])
            chunks = chunks_of(factors[tree_level].shape[1])

            def produce(chunk, side, after):
                vector = last
                if after is not None:
                    vector, _ = tied(vector, after)
                return apply_rows(
                    *matrix_of("coupling", tree_level, plane), vector, early.get(tree_level), chunk, side, chunks
                )

            factor = factors[tree_level]
            count = factor.shape[1] // chunks // 2

            def consume(parts, state, final):
                noise_held = ("noise", tree_level) in held
                noise = held["noise", tree_level] if noise_held else noises[tree_level]
                return across_rows(
                    *matrix_of("factor", tree_level, 0), parts, count, noise=noise, noise_held=noise_held,
                    base=state, final=final,
                )

            part, _ = rows_stage(produce, consume, chunks, waits, True)
        if tree_level == 0:
            waits = work([], [], [load_job(("coupling", 1), 0), load_job(("factor", 1), 0, True)])
        elif tree_level == 1:
            waits = work(
                [early_job(3, 0, last)],
                [early_job(2, 0, last), load_job(("coupling", 2), 1)],
            )
        elif tree_level == 2:
            waits = work([load_job(("coupling", 3), 2)])
        else:
            waits = work()
        samples.append(group_sum(part, group_bits, leaf_index, waits))
        waits.drain()

    losses = []

    def loss_job(given):
        total = jnp.zeros((8, scenario_count), jnp.float32)
        for tree_level in range(LEVELS):
            group_bits = leaf_bits - tree_level
            piece_rows = given[tree_level].shape[0] >> group_bits
            member = leaf_index & (1 << group_bits) - 1
            own_rows = lax.dynamic_slice_in_dim(given[tree_level], member * piece_rows, piece_rows, 0)
            terms = weights[None, :] * jax.nn.softplus(own_rows - tail_level)
            total = total + jnp.sum(terms.reshape(-1, 8, scenario_count), axis=0)
        return total

    steps = [("leaf", position) for position in range(leaf_bits)]
    steps += [("rows", position) for position in range(bits_of("rows"))]

    def sum_job(count):
        def run(given):
            for _ in range(count):
                if steps:
                    axis, position = steps.pop(0)
                    given = given + swapped(given, axis, position)
            return given

        return (lambda: losses[-1], run, losses.append)

    pending = [None] * LEVELS
    gradients = [None] * LEVELS

    def later_job(level, plane):
        places = [(chunk, side) for _, chunk, side in solved[level]]

        def run(given):
            parts = [(terms, chunk, side) for terms, (chunk, side) in zip(given, places)]
            return across_rows(
                couplings[level][0], plane, parts, given[0].shape[0], extra=pending[plane]
            )

        return (
            lambda: [terms for terms, _, _ in solved[level]],
            run,
            lambda result: pending.__setitem__(plane, result),
        )

    def tail_run(given):
        rows, ticket = given
        total = jnp.sum(sum_job(len(steps))[1](rows) + ticket)
        return total / jnp.float32(
            (2**LEVELS - 1) * full_width * (scenario_count + tail_index.shape[0])
        )

    tail_job = (lambda: (losses[-1], tickets[-1]), tail_run, losses.append)
    solved = {}
    for name in list(held):
        if name != ("factor", 3):
            del held[name]
    loss_start = (lambda: samples, lambda given: sum_job(2)[1](loss_job(given)), losses.append)
    for tree_level in reversed(range(LEVELS)):
        group_bits = leaf_bits - tree_level
        adjoint = weights[None, :] * jax.nn.sigmoid(samples[tree_level] - tail_level)
        if tree_level < LEVELS - 1:
            if tree_level == 2:
                waits = work(
                    [
                        later_job(3, 1), load_job(("factor", 2), 0),
                    ]
                )
            elif tree_level == 1:
                waits = work(
                    [later_job(2, 0)], [load_job(("factor", 1), 0)]
                )
            else:
                waits = work([], [], [load_job(("factor", 0), 0)])
            adjoint = adjoint - group_sum(pending[tree_level], group_bits, leaf_index, waits)
            waits.drain()
        adjoint_round = adjoint.astype(jnp.bfloat16)
        chunks = chunks_of(factors[tree_level].shape[1])
        if tree_level == 3:
            waits = work([load_job(("coupling", 3), 2), loss_start])
        elif tree_level == 2:
            waits = work([later_job(3, 0), load_job(("coupling", 2), 1), sum_job(2)])
        elif tree_level == 1:
            waits = work([load_job(("coupling", 1), 0), sum_job(1)])
        else:
            waits = work([tail_job])

        def produce(chunk, side, after):
            vector = adjoint_round
            if after is not None:
                vector, _ = tied(vector, after)
            place = matrix_of("factor", tree_level, 0)
            if chunk > 0 and side == 0:
                place = (factors[tree_level], 0)
            return apply_rows(*place, vector, None, chunk, side, chunks)

        count = factors[tree_level].shape[1] // chunks // 2

        def consume(parts, state, final):
            if tree_level == 0:
                return ()
            base, exact = (None, None) if state is None else state
            return across_rows(
                *matrix_of("coupling", tree_level, tree_level - 1), parts, count,
                base=base, extra=pending[tree_level - 1] if final else None, exact=exact, give_exact=True,
                final=final,
            )

        state, solved[tree_level] = rows_stage(produce, consume, chunks, waits, False)
        if tree_level == 0:
            gradients[0] = place_rows(*[terms for terms, _, _ in solved[0]])
            continue
        pending[tree_level - 1], gradients[tree_level] = state
    return (gradients[0], gradients[1], gradients[2], gradients[3], losses[-1])


def solution(mesh):
    in_specs = (
        P("leaf", "rows"),
        P("leaf", "rows"),
        P("leaf", "rows"),
        P("leaf", "rows"),
        P("leaf", None, "rows"),
        P("leaf", None, "rows"),
        P("leaf", None, "rows"),
        P("leaf", None),
        P("leaf", None),
        P("leaf", None),
        P("leaf", None),
        P(),
    )
    out_specs = (P("leaf", None), P("leaf", None), P("leaf", None), P("leaf", None), P())
    return jax.shard_map(
        on_device, mesh=mesh, in_specs=in_specs, out_specs=out_specs, check_vma=False
    )
```
